256 devices in a mesh: gz: 8 (over x, core), ma: 32 (over z, y).
Axes of the slice: x: 4, y: 4, z: 8, core: 2. Of those that a mesh axis runs over, the one named last changes fastest.
Arguments:
- forward: float32 [8, 2, 1024, 4096], P('gz', None, 'ma'), may hold values from -6 to 6
- cotangent: float32 [8, 2, 1024, 4096], P('gz', None, 'ma'), may hold values from -6 to 6
- mode_order: int32 [1024], replicated, may hold values from 0 to 1023, each once
- region: int32 [128, 128], replicated, may hold values from 0 to 7
- chi: float32 [8], replicated, may hold values from 0.5 to 2
- phase: float32 [1024, 4096], P('ma'), may hold values from -3.140625 to 3.140625
- loss: float32 [8, 1024], P('gz', 'ma'), may hold values from 0.5 to 1
Outputs:
- adjoint: float32 [8, 2, 1024, 4096], P('gz', None, 'ma')
The draws below stay inside these ranges and needn't reach their ends.
Inputs may be any that keep to these rules, and one draw needn't show every extreme that they name: Each number appears once; stored mode m has order mode_order[m] // 32 along the first transverse coordinate and mode_order[m] % 32 along the second.
All inputs are finite; a program needn't handle non-finite values.
Results may differ from the reference program's by a relative error of at most 0.0003.
Values sent between devices are 32-bit elements; how exact they have to be, the bound alone decides.
No kernel may reach another device: no remote copies, remote signals or barrier semaphores. Data moves between devices by JAX's collectives and lax.ppermute only.
A program may use at most 128 MiB of HBM per device.

```python
import math
import jax
import jax.numpy as jnp
from jax import lax

HG_ORDER = 32
MODES = 1024
TIME = 4096
GRID = 128
REGIONS = 8
ZL = 8
N_MA = 32


def with_ends(array, stream_key, smallest, top_value):
    longest = array.shape.index(max(array.shape))
    spots = []
    for shift in (0, 1):
        where = [jax.random.randint(jax.random.fold_in(stream_key, axis), (), 0, length) for axis, length in enumerate(array.shape)]
        where[longest] = (where[longest] + shift) % array.shape[longest]
        spots.append(tuple(where))
    return array.at[spots[0]].set(smallest).at[spots[1]].set(top_value)


def block_scale(key, dims, split, smallest, largest):
    factor_of, own = 1.0, jax.random.fold_in(key, 6)
    for axis_at, shards_of in split:
        heights = jnp.exp(jax.random.uniform(jax.random.fold_in(own, axis_at), (shards_of,), jnp.float32, smallest / len(split), largest / len(split)))
        factor_of = factor_of * jnp.repeat(heights, dims[axis_at] // shards_of).reshape([-1 if axis == axis_at else 1 for axis in range(len(dims))])
    return factor_of


def scatter_about(rng, shape, width, bound, split=(), kind=jnp.bfloat16):
    entries = width * jax.random.normal(rng, shape, jnp.float32)
    if split:
        entries = entries * block_scale(rng, shape, split, -0.22, 0.18)
    return jnp.clip(entries, -bound, bound).astype(kind)


def setup_inputs(seed: int = 0) -> dict:
    splits = jax.random.split(jax.random.key(seed), 8)
    return {
        "forward": scatter_about(splits[0], (ZL, 2, MODES, TIME), 1.0, 6.0, ((0, 8), (2, 32)), jnp.float32),
        "cotangent": scatter_about(splits[1], (ZL, 2, MODES, TIME), 1.0, 6.0, ((0, 8), (2, 32)), jnp.float32),
        "mode_order": jax.random.permutation(splits[2], MODES).astype(jnp.int32),
        "region": with_ends(jax.random.randint(splits[3], (GRID, GRID), 0, REGIONS), jax.random.fold_in(splits[3], 1), 0, REGIONS - 1).astype(jnp.int32),
        "chi": jnp.clip(jnp.exp(jax.random.uniform(splits[4], (REGIONS,), jnp.float32, math.log(0.5), math.log(2.0))), 0.5, 2.0),
        "phase": jnp.clip(jax.random.uniform(splits[5], (MODES, TIME), jnp.float32, -3.140625, 3.140625), -3.140625, 3.140625),
        "loss": jnp.clip(0.5 + 0.5 * jax.random.uniform(splits[6], (ZL, MODES), jnp.float32) ** block_scale(splits[6], (ZL, MODES), ((0, 8), (1, 32)), -0.2, 0.2), 0.5, 1.0),
    }


gamma_kerr = 2.0
half_width = 10.0

def hermite_table(grid_points, degrees):
    spacing = 2.0 * half_width / grid_points
    coords = (jnp.arange(grid_points, dtype=jnp.float32) - (grid_points - 1) / 2.0) * spacing
    columns = [jnp.exp(-0.5 * coords * coords) * math.pi ** (-0.25)]
    if degrees > 1:
        columns.append(math.sqrt(2.0) * coords * columns[0])
    for degree in range(2, degrees):
        following = math.sqrt(2.0 / degree) * coords * columns[degree - 1] - math.sqrt((degree - 1.0) / degree) * columns[degree - 2]
        columns.append(following)
    return jnp.stack(columns, axis=1) * math.sqrt(spacing)

def modes_to_grid(fields, table):
    partial_grid = jnp.einsum('...pqt,yq->...pyt', fields, table, precision=lax.Precision.HIGHEST)
    return jnp.einsum('...pyt,xp->...xyt', partial_grid, table, precision=lax.Precision.HIGHEST)

def grid_to_modes(values, table):
    partial_grid = jnp.einsum('...xyt,xp->...pyt', values, table, precision=lax.Precision.HIGHEST)
    return jnp.einsum('...pyt,yq->...pqt', partial_grid, table, precision=lax.Precision.HIGHEST)

def kerr_adjoint(forward, cotangent, table, chi_grid, inverse, mode_order):
    leading = forward.shape[:-2]
    samples = forward.shape[-1]
    degrees = table.shape[1]

    def ordered_grid(fields):
        ordered = jnp.take(fields, inverse, axis=-2)
        return ordered.reshape(leading + (degrees, degrees, samples))
    field_grid = modes_to_grid(ordered_grid(forward), table)
    cot_grid = modes_to_grid(ordered_grid(cotangent), table)
    field_real = field_grid[..., 0, :, :, :]
    field_imag = field_grid[..., 1, :, :, :]
    cot_real = cot_grid[..., 0, :, :, :]
    cot_imag = cot_grid[..., 1, :, :, :]
    strength = gamma_kerr * chi_grid[:, :, None]
    intensity = field_real * field_real + field_imag * field_imag
    cross = 2.0 * field_real * field_imag
    grad_real = strength * (-cross * cot_real + (intensity + 2.0 * field_real * field_real) * cot_imag)
    grad_imag = strength * (-(intensity + 2.0 * field_imag * field_imag) * cot_real + cross * cot_imag)
    projected = grid_to_modes(jnp.stack([grad_real, grad_imag], axis=-4), table)
    flat = projected.reshape(leading + (degrees * degrees, samples))
    return jnp.take(flat, mode_order, axis=-2)

def reference(forward, cotangent, mode_order, region, chi, phase, loss):
    table = hermite_table(GRID, HG_ORDER)
    matches = (region[:, :, None] == jnp.arange(REGIONS, dtype=jnp.int32)[None, None, :]).astype(jnp.float32)
    chi_grid = lax.optimization_barrier(jnp.sum(matches * chi[None, None, :], axis=-1))
    inverse = jnp.zeros((MODES,), jnp.int32).at[mode_order].set(jnp.arange(MODES, dtype=jnp.int32))
    block_size = TIME // N_MA

    def one_block(block_index):
        start = (block_index * block_size).astype(jnp.int32)
        forward_block = lax.dynamic_slice_in_dim(forward, start, block_size, 3)
        cot_block = lax.dynamic_slice_in_dim(cotangent, start, block_size, 3)
        return kerr_adjoint(forward_block, cot_block, table, chi_grid, inverse, mode_order)
    pieces = lax.map(one_block, jnp.arange(N_MA, dtype=jnp.int32))
    kerr = jnp.moveaxis(pieces, 0, 3).reshape(ZL, 2, MODES, TIME)
    source = cotangent + kerr
    wave = lax.complex(source[:, 0], source[:, 1])
    spectrum = jnp.fft.fft(wave, axis=-1) * lax.complex(jnp.cos(phase), -jnp.sin(phase))[None]
    back = jnp.fft.ifft(spectrum, axis=-1)
    dispersed = jnp.stack([jnp.real(back), jnp.imag(back)], axis=1)

    def backward_step(carry, inputs):
        term, factor = inputs
        value = term + factor[None, :, None] * carry
        return (value, value)
    start_carry = jnp.zeros_like(dispersed[0])
    final_carry, adjoint = lax.scan(backward_step, start_carry, (dispersed, loss), reverse=True)
    return adjoint
```

```python
import math

import jax
import jax.numpy as jnp
import numpy as np
from jax import lax
from jax.experimental import pallas as pl
from jax.experimental.pallas import tpu as pltpu
from jax.sharding import PartitionSpec as P

ORDER = 32
MODES = 1024
GRID = 128
REGIONS = 8
TIME = 4096
BLOCK = 128
OUTER = 32
ZL = 8
PER = 4
BF = jnp.bfloat16
F32 = jnp.float32


def hermite_table():
    step = 20.0 / GRID
    coords = (np.arange(GRID, dtype=np.float64) - (GRID - 1) / 2.0) * step
    columns = [np.exp(-0.5 * coords * coords) * math.pi ** (-0.25)]
    columns.append(math.sqrt(2.0) * coords * columns[0])
    for n in range(2, ORDER):
        columns.append(
            math.sqrt(2.0 / n) * coords * columns[n - 1]
            - math.sqrt((n - 1.0) / n) * columns[n - 2]
        )
    return np.stack(columns, axis=1) * math.sqrt(step)


def halves(array):
    head = array.astype(jnp.bfloat16)
    tail = (array - head.astype(np.float64)).astype(jnp.bfloat16)
    return head, tail


def split(value):
    head = value.astype(BF)
    return head, (value - head.astype(F32)).astype(BF)


def dot(a, b):
    return jnp.dot(a, b, preferred_element_type=F32)


def kerr_kernel(x_ref, place_ref, back_ref, fwd_ref, proj_ref, tt_ref, k_ref, o_ref,
                xs, fs, gs, rs, ks):
    def split_in(j, carry):
        rows = pl.ds(pl.multiple_of(j * 32, 32), 32)
        for f in range(4):
            head, tail = split(x_ref[j, f])
            xs[f, rows, 0:128] = head
            xs[f, rows, 128:256] = tail
        return carry

    lax.fori_loop(0, 32, split_in, 0, unroll=4)

    def place(f, carry):
        fs[f] = dot(place_ref[...], xs[f]).astype(BF)
        return carry

    lax.fori_loop(0, 4, place, 0)

    def first(p, carry):
        rows = pl.ds(pl.multiple_of(p * 32, 32), 32)
        out_rows = pl.ds(pl.multiple_of(p * 128, 128), 128)
        for pair in range(2):
            a, b = fs[2 * pair, rows, :], fs[2 * pair + 1, rows, :]
            head = jnp.concatenate([a[:, :128], b[:, :128]], axis=1)
            tail = jnp.concatenate([a[:, 128:], b[:, 128:]], axis=1)
            got = dot(fwd_ref[...], jnp.concatenate([head, tail, head], axis=0))
            gs[2 * pair, out_rows, :] = got[:, :128]
            gs[2 * pair + 1, out_rows, :] = got[:, 128:]
        return carry

    lax.fori_loop(0, 32, first, 0, unroll=2)

    def column(y, carry):
        fields = []
        for pair in range(2):
            got = [split(gs[2 * pair + c, pl.ds(y, 32, stride=128), :]) for c in range(2)]
            head = jnp.concatenate([got[0][0], got[1][0]], axis=1)
            tail = jnp.concatenate([got[0][1], got[1][1]], axis=1)
            fields.append(dot(fwd_ref[...], jnp.concatenate([head, tail, head], axis=0)))
        er, ei = fields[0][:, :128], fields[0][:, 128:]
        cr, ci = fields[1][:, :128], fields[1][:, 128:]
        rr, ii, ri = er * er, ei * ei, er * ei
        cross = ri + ri
        total = rr + ii
        gr = (total + (rr + rr)) * ci - cross * cr
        gi = cross * ci - (total + (ii + ii)) * cr
        gr_h, gr_l = split(gr)
        gi_h, gi_l = split(gi)
        right = jnp.concatenate(
            [jnp.concatenate([gr_h, gi_h], axis=1), jnp.concatenate([gr_l, gi_l], axis=1)], axis=0
        )
        t_h, t_l = split(tt_ref[...] * k_ref[pl.ds(y, 1), :])
        left = jnp.concatenate(
            [jnp.concatenate([t_h, t_h], axis=1), jnp.concatenate([t_l, jnp.zeros_like(t_l)], axis=1)],
            axis=0,
        )
        got = dot(left, right)
        got = got[:32] + got[32:]
        rows = pl.ds(pl.multiple_of(y * 32, 32), 32)
        rs[0, rows, :] = got[:, :128]
        rs[1, rows, :] = got[:, 128:]
        return carry

    lax.fori_loop(0, GRID, column, 0, unroll=2)

    def last(p, carry):
        got = [split(rs[c, pl.ds(p, 128, stride=32), :]) for c in range(2)]
        right = jnp.concatenate(
            [jnp.concatenate([got[0][i], got[1][i]], axis=1) for i in range(2)], axis=0
        )
        res = dot(proj_ref[...], right)
        res = res[:32] + res[32:]
        rows = pl.ds(pl.multiple_of(p * 32, 32), 32)
        for c in range(2):
            head, tail = split(res[:, c * 128:(c + 1) * 128])
            ks[c, rows, 0:128] = head
            ks[c, rows, 128:256] = tail
        return carry

    lax.fori_loop(0, 32, last, 0, unroll=2)

    def finish(j, carry):
        rows = pl.ds(pl.multiple_of(j * 256, 256), 256)
        for c in range(2):
            res = dot(back_ref[rows, :], ks[c])
            res = res[:, :128] + res[:, 128:]
            for i in range(8):
                value = res[i * 32:(i + 1) * 32] + x_ref[j * 8 + i, 2 + c]
                for g in range(8):
                    o_ref[g, j * 8 + i, c * 4:(c + 1) * 4, :] = value[g * 4:(g + 1) * 4]
        return carry

    lax.fori_loop(0, 4, finish, 0)


def kerr_call(received, place, back, fwd, proj, tt, k):
    vm = pl.BlockSpec(memory_space=pltpu.VMEM)
    return pl.pallas_call(
        kerr_kernel,
        name="kerr",
        out_shape=jax.ShapeDtypeStruct((ZL, 32, 8, 128), F32),
        in_specs=[vm] * 7,
        out_specs=vm,
        scratch_shapes=[
            pltpu.VMEM((4, MODES, 256), BF),
            pltpu.VMEM((4, MODES, 256), BF),
            pltpu.VMEM((4, ORDER * GRID, 128), F32),
            pltpu.VMEM((2, ORDER * GRID, 128), F32),
            pltpu.VMEM((2, MODES, 256), BF),
        ],
        compiler_params=pltpu.CompilerParams(vmem_limit_bytes=48 * 2**20),
        cost_estimate=pl.CostEstimate(flops=2 * 10**10, bytes_accessed=8 * 2**20, transcendentals=0),
    )(received, place, back, fwd, proj, tt, k)


def three(a_h, a_l, b_h, b_l):
    return dot(a_h, b_h) + (dot(a_h, b_l) + dot(a_l, b_h))


def spectral_kernel(s_ref, l_ref, ph_ref, w1_ref, w2_ref, w3_ref, w4_ref, tw_ref, o_ref, sc):
    for z in range(ZL - 1, -1, -1):
        if z == ZL - 1:
            sc[z] = s_ref[z]
        else:
            sc[z] = s_ref[z] + l_ref[z] * sc[z + 1]
    tw_r = jnp.concatenate([tw_ref[0]] * PER, axis=0)
    tw_i = jnp.concatenate([tw_ref[1]] * PER, axis=0)
    ph_r, ph_i = ph_ref[0], ph_ref[1]

    def pair(j, carry):
        z0 = 2 * j
        a = jnp.concatenate(
            [sc[z0].reshape(256, 128), sc[z0 + 1].reshape(256, 128)], axis=1
        )
        a_h, a_l = split(a)
        first = three(w1_ref[0], w1_ref[1], a_h, a_l)
        outs = []
        for i in range(2):
            re, im = first[:128, i * 128:(i + 1) * 128], first[128:, i * 128:(i + 1) * 128]
            seg = jnp.concatenate([re * tw_r - im * tw_i, re * tw_i + im * tw_r], axis=1)
            s_h, s_l = split(seg)
            spec = three(s_h, s_l, w2_ref[0], w2_ref[1])
            re, im = spec[:, :128], spec[:, 128:]
            spec = jnp.concatenate([re * ph_r - im * ph_i, re * ph_i + im * ph_r], axis=1)
            s_h, s_l = split(spec)
            seg = three(s_h, s_l, w3_ref[0], w3_ref[1])
            re, im = seg[:, :128], seg[:, 128:]
            outs.append(
                jnp.concatenate([re * tw_r + im * tw_i, im * tw_r - re * tw_i], axis=0)
            )
        b_h, b_l = split(jnp.concatenate(outs, axis=1))
        final = three(w4_ref[0], w4_ref[1], b_h, b_l)
        o_ref[z0] = final[:, :128]
        o_ref[z0 + 1] = final[:, 128:]
        return carry

    lax.fori_loop(0, ZL // 2, pair, 0)


def spectral_constants():
    a = np.arange(OUTER)
    ang1 = 2 * math.pi / OUTER * (np.outer(a, a) % OUTER)
    c1, s1 = np.cos(ang1), np.sin(ang1)
    eye = np.eye(PER)
    w1 = np.zeros((2, PER, OUTER, OUTER, 2, PER))
    blocks = {(0, 0): c1, (0, 1): s1, (1, 0): -s1, (1, 1): c1}
    for (co, ci), m in blocks.items():
        w1[co, :, :, :, ci, :] = np.einsum("mn,ka->mkan", eye, m)
    w1 = w1.reshape(256, 256)
    w4 = np.zeros((OUTER, 2, PER, 2, PER, OUTER))
    blocks = {(0, 0): c1, (0, 1): -s1, (1, 0): s1, (1, 1): c1}
    for (co, ci), m in blocks.items():
        w4[:, co, :, ci, :, :] = np.einsum("mn,ka->amnk", eye, m)
    w4 = w4.reshape(256, 256) / TIME
    b = np.arange(BLOCK)
    ang2 = 2 * math.pi / BLOCK * (np.outer(b, b) % BLOCK)
    c2, s2 = np.cos(ang2), np.sin(ang2)
    w2 = np.block([[c2, -s2], [s2, c2]])
    w3 = np.block([[c2, s2], [-s2, c2]])
    angt = 2 * math.pi / TIME * (np.outer(a, b) % TIME)
    tw = np.stack([np.cos(angt), -np.sin(angt)]).astype(np.float32)
    return [np.stack(halves(w)) for w in (w1, w2, w3, w4)] + [tw]


def spectral_call(source, factors, turn):
    w1, w2, w3, w4, tw = spectral_constants()
    vm = pl.BlockSpec(memory_space=pltpu.VMEM)
    return pl.pallas_call(
        spectral_kernel,
        name="spectral",
        out_shape=jax.ShapeDtypeStruct((ZL, 256, 128), F32),
        in_specs=[vm] * 8,
        out_specs=vm,
        scratch_shapes=[pltpu.VMEM((ZL, OUTER, 8, 128), F32)],
        compiler_params=pltpu.CompilerParams(vmem_limit_bytes=32 * 2**20),
        cost_estimate=pl.CostEstimate(flops=3 * 10**9, bytes_accessed=4 * 2**20, transcendentals=0),
    )(source, factors, turn, w1, w2, w3, w4, tw)


def gathered_loss(loss):
    size = lax.axis_size("gz")
    have = loss
    reach = 1
    while reach < size:
        route = [((i + reach) % size, i) for i in range(size)]
        have = jnp.concatenate([have, lax.ppermute(have, "gz", route)], axis=0)
        reach *= 2
    me = lax.axis_index("gz")
    return lax.dynamic_slice_in_dim(jnp.concatenate([have, have], axis=0), size - me, size, 0)


def kerr_constants(mode_order, region, chi):
    t = hermite_table()
    t_h, t_l = halves(t)
    fwd = np.concatenate([t_h, t_h, t_l], axis=1)
    proj = np.concatenate(
        [np.concatenate([t_h.T, t_h.T], axis=1), np.concatenate([t_l.T, np.zeros_like(t_l.T)], axis=1)],
        axis=0,
    )
    tt = np.ascontiguousarray(t.T).astype(np.float32)
    matches = (region[None, :, :] == jnp.arange(REGIONS, dtype=jnp.int32)[:, None, None]).astype(F32)
    k = 2.0 * jnp.sum(matches * chi[:, None, None], axis=0).T
    index = jnp.arange(MODES, dtype=jnp.int32)
    place = (index[:, None] == mode_order[None, :]).astype(BF)
    back = (mode_order[:, None] == index[None, :]).astype(BF)
    return place, back, fwd, proj, tt, k


def on_device(forward, cotangent, mode_order, region, chi, phase, loss):
    me = lax.axis_index("gz")
    both = jnp.concatenate([forward[0], cotangent[0]], axis=0)
    send = both.reshape(4, 32, 32, BLOCK).transpose(2, 0, 1, 3)
    received = lax.all_to_all(send, "ma", split_axis=0, concat_axis=0, tiled=True)
    constants = kerr_constants(mode_order, region, chi)
    source = kerr_call(received, *constants)
    source = source.reshape(256, 8, 128)
    gathered = lax.all_to_all(source, ("gz", "ma"), split_axis=0, concat_axis=0, tiled=True)
    factors = lax.dynamic_slice_in_dim(gathered_loss(loss), me * PER, PER, 1)
    factors = jnp.concatenate([factors, factors], axis=1)
    factors = jnp.broadcast_to(factors[:, None, :, None], (ZL, 1, 8, 128))
    angles = lax.dynamic_slice_in_dim(phase, me * PER, PER, 0)
    angles = angles.reshape(PER, BLOCK, OUTER).transpose(0, 2, 1).reshape(PER * OUTER, BLOCK)
    turn = jnp.stack([jnp.cos(angles), -jnp.sin(angles)])
    result = spectral_call(gathered.reshape(ZL, OUTER, 8, 128), factors, turn)
    result = lax.all_to_all(result, "gz", split_axis=0, concat_axis=0, tiled=True)
    result = result.reshape(8, OUTER, 2, PER, BLOCK).transpose(2, 0, 3, 1, 4)
    return result.reshape(1, 2, 32, TIME)


def solution(mesh):
    in_specs = (
        P("gz", None, "ma", None),
        P("gz", None, "ma", None),
        P(),
        P(),
        P(),
        P("ma", None),
        P("gz", "ma"),
    )
    return jax.shard_map(
        on_device, mesh=mesh, in_specs=in_specs, out_specs=P("gz", None, "ma", None), check_vma=False
    )
```

```python
import math

import jax
import jax.numpy as jnp
import numpy as np
from jax import lax
from jax.experimental import pallas as pl
from jax.experimental.pallas import tpu as pltpu
from jax.sharding import PartitionSpec as P

ORDER = 32
MODES = 1024
GRID = 128
REGIONS = 8
TIME = 4096
BLOCK = 128
OUTER = 32
ZL = 8
PER = 4
BF = jnp.bfloat16
F32 = jnp.float32


def hermite_table():
    step = 20.0 / GRID
    coords = (np.arange(GRID, dtype=np.float64) - (GRID - 1) / 2.0) * step
    columns = [np.exp(-0.5 * coords * coords) * math.pi ** (-0.25)]
    columns.append(math.sqrt(2.0) * coords * columns[0])
    for n in range(2, ORDER):
        columns.append(
            math.sqrt(2.0 / n) * coords * columns[n - 1]
            - math.sqrt((n - 1.0) / n) * columns[n - 2]
        )
    return np.stack(columns, axis=1) * math.sqrt(step)


def halves(array):
    head = array.astype(jnp.bfloat16)
    tail = (array - head.astype(np.float64)).astype(jnp.bfloat16)
    return head, tail


def split(value):
    head = value.astype(BF)
    return head, (value - head.astype(F32)).astype(BF)


def dot(a, b):
    return jnp.dot(a, b, preferred_element_type=F32)


def kerr_kernel(x_ref, place_ref, back_ref, f2_ref, f3_ref, proj_ref, tt_ref, k_ref, o_ref,
                xs, fs, gs, rs, ks):
    def split_in(j, carry):
        rows = pl.ds(pl.multiple_of(j * 32, 32), 32)
        for f in range(4):
            head, tail = split(x_ref[j, f])
            xs[f, rows, 0:128] = head
            xs[f, rows, 128:256] = tail
        return carry

    lax.fori_loop(0, 32, split_in, 0, unroll=4)

    def place(f, carry):
        fs[f] = dot(place_ref[...], xs[f]).astype(BF)
        return carry

    lax.fori_loop(0, 4, place, 0)

    def first(k, carry):
        for pair in range(2):
            got = []
            for h in range(2):
                rows = pl.ds(pl.multiple_of(k * 128 + h * 64, 64), 64)
                a, b = fs[2 * pair, rows, :], fs[2 * pair + 1, rows, :]
                head = jnp.concatenate([a[:, :128], b[:, :128]], axis=1)
                tail = jnp.concatenate([a[:, 128:], b[:, 128:]], axis=1)
                res = dot(f2_ref[...], jnp.concatenate([head, tail, head], axis=0))
                got.append(res.reshape(32, 8, 256))
            low = jnp.concatenate([got[0][:, :4], got[1][:, :4]], axis=1)
            high = jnp.concatenate([got[0][:, 4:], got[1][:, 4:]], axis=1)
            for c in range(2):
                lanes = slice(c * 128, (c + 1) * 128)
                gs[2 * pair + c, :, 0, k] = low[:, :, lanes]
                gs[2 * pair + c, :, 1, k] = high[:, :, lanes]
        return carry

    lax.fori_loop(0, 8, first, 0)

    def column(v, parity):
        u = 2 * v + parity
        fields = []
        for pair in range(2):
            got = [split(gs[2 * pair + c, v, parity].reshape(64, 128)) for c in range(2)]
            head = jnp.concatenate([got[0][0], got[1][0]], axis=1)
            tail = jnp.concatenate([got[0][1], got[1][1]], axis=1)
            fields.append(dot(f3_ref[...], jnp.concatenate([head, tail, head], axis=0)))
        res = []
        for i in range(2):
            xr = slice(i * 128, (i + 1) * 128)
            er, ei = fields[0][xr, :128], fields[0][xr, 128:]
            cr, ci = fields[1][xr, :128], fields[1][xr, 128:]
            total = er * er + ei * ei
            turn = er * ci - ei * cr
            turn = turn + turn
            gr_h, gr_l = split(total * ci + turn * er)
            gi_h, gi_l = split(turn * ei - total * cr)
            right = jnp.concatenate(
                [jnp.concatenate([gr_h, gi_h], axis=1), jnp.concatenate([gr_l, gi_l], axis=1)], axis=0
            )
            t_h, t_l = split(tt_ref[...] * k_ref[pl.ds(2 * u + i, 1), :])
            left = jnp.concatenate(
                [
                    jnp.concatenate([t_h, t_h], axis=1),
                    jnp.concatenate([t_l, jnp.zeros_like(t_l)], axis=1),
                ],
                axis=0,
            )
            got = dot(left, right)
            res.append(got[:32] + got[32:])
        rows = pl.ds(pl.multiple_of(u * 16, 16), 16)
        for g in range(4):
            both = jnp.concatenate([res[i][g * 8:(g + 1) * 8] for i in range(2)], axis=0)
            head, tail = split(both)
            rs[0, g, rows, :] = head
            rs[1, g, rows, :] = tail

    def columns(v, carry):
        column(v, 0)
        column(v, 1)
        return carry

    lax.fori_loop(0, GRID // 4, columns, 0)

    def last(g, carry):
        head, tail = rs[0, g], rs[1, g]
        res = dot(proj_ref[0], head) + (dot(proj_ref[0], tail) + dot(proj_ref[1], head))
        rows = pl.ds(pl.multiple_of(g * 256, 256), 256)
        for c in range(2):
            head, tail = split(res[:, c * 128:(c + 1) * 128])
            ks[c, rows, 0:128] = head
            ks[c, rows, 128:256] = tail
        return carry

    lax.fori_loop(0, 4, last, 0)

    def finish(j, carry):
        rows = pl.ds(pl.multiple_of(j * 256, 256), 256)
        for c in range(2):
            res = dot(back_ref[rows, :], ks[c])
            res = res[:, :128] + res[:, 128:]
            for i in range(8):
                value = res[i * 32:(i + 1) * 32] + x_ref[j * 8 + i, 2 + c]
                for g in range(8):
                    o_ref[g, j * 8 + i, c * 4:(c + 1) * 4, :] = value[g * 4:(g + 1) * 4]
        return carry

    lax.fori_loop(0, 4, finish, 0)


def kerr_call(received, *constants):
    vm = pl.BlockSpec(memory_space=pltpu.VMEM)
    return pl.pallas_call(
        kerr_kernel,
        name="kerr",
        out_shape=jax.ShapeDtypeStruct((ZL, 32, 8, 128), F32),
        in_specs=[vm] * (1 + len(constants)),
        out_specs=vm,
        scratch_shapes=[
            pltpu.VMEM((4, MODES, 256), BF),
            pltpu.VMEM((4, MODES, 256), BF),
            pltpu.VMEM((4, 32, 2, 8, 8, 128), F32),
            pltpu.VMEM((2, 4, MODES, 256), BF),
            pltpu.VMEM((2, MODES, 256), BF),
        ],
        compiler_params=pltpu.CompilerParams(vmem_limit_bytes=48 * 2**20),
        cost_estimate=pl.CostEstimate(flops=2 * 10**10, bytes_accessed=8 * 2**20, transcendentals=0),
    )(received, *constants)


def three(a_h, a_l, b_h, b_l):
    return dot(a_h, b_h) + (dot(a_h, b_l) + dot(a_l, b_h))


def spectral_kernel(s_ref, l_ref, ph_ref, w1_ref, w2_ref, w3_ref, w4_ref, tw_ref, o_ref, sc):
    for z in range(ZL - 1, -1, -1):
        if z == ZL - 1:
            sc[z] = s_ref[z]
        else:
            sc[z] = s_ref[z] + l_ref[z] * sc[z + 1]
    tw_r = jnp.concatenate([tw_ref[0]] * PER, axis=0)
    tw_i = jnp.concatenate([tw_ref[1]] * PER, axis=0)
    ph_r, ph_i = ph_ref[0], ph_ref[1]

    def pair(j, carry):
        z0 = 2 * j
        a = jnp.concatenate(
            [sc[z0].reshape(256, 128), sc[z0 + 1].reshape(256, 128)], axis=1
        )
        a_h, a_l = split(a)
        first = three(w1_ref[0], w1_ref[1], a_h, a_l)
        outs = []
        for i in range(2):
            re, im = first[:128, i * 128:(i + 1) * 128], first[128:, i * 128:(i + 1) * 128]
            seg = jnp.concatenate([re * tw_r - im * tw_i, re * tw_i + im * tw_r], axis=1)
            s_h, s_l = split(seg)
            spec = three(s_h, s_l, w2_ref[0], w2_ref[1])
            re, im = spec[:, :128], spec[:, 128:]
            spec = jnp.concatenate([re * ph_r - im * ph_i, re * ph_i + im * ph_r], axis=1)
            s_h, s_l = split(spec)
            seg = three(s_h, s_l, w3_ref[0], w3_ref[1])
            re, im = seg[:, :128], seg[:, 128:]
            outs.append(
                jnp.concatenate([re * tw_r + im * tw_i, im * tw_r - re * tw_i], axis=0)
            )
        b_h, b_l = split(jnp.concatenate(outs, axis=1))
        final = three(w4_ref[0], w4_ref[1], b_h, b_l)
        o_ref[z0] = final[:, :128]
        o_ref[z0 + 1] = final[:, 128:]
        return carry

    lax.fori_loop(0, ZL // 2, pair, 0)


def spectral_constants():
    a = np.arange(OUTER)
    ang1 = 2 * math.pi / OUTER * (np.outer(a, a) % OUTER)
    c1, s1 = np.cos(ang1), np.sin(ang1)
    eye = np.eye(PER)
    w1 = np.zeros((2, PER, OUTER, OUTER, 2, PER))
    blocks = {(0, 0): c1, (0, 1): s1, (1, 0): -s1, (1, 1): c1}
    for (co, ci), m in blocks.items():
        w1[co, :, :, :, ci, :] = np.einsum("mn,ka->mkan", eye, m)
    w1 = w1.reshape(256, 256)
    w4 = np.zeros((OUTER, 2, PER, 2, PER, OUTER))
    blocks = {(0, 0): c1, (0, 1): -s1, (1, 0): s1, (1, 1): c1}
    for (co, ci), m in blocks.items():
        w4[:, co, :, ci, :, :] = np.einsum("mn,ka->amnk", eye, m)
    w4 = w4.reshape(256, 256) / TIME
    b = np.arange(BLOCK)
    ang2 = 2 * math.pi / BLOCK * (np.outer(b, b) % BLOCK)
    c2, s2 = np.cos(ang2), np.sin(ang2)
    w2 = np.block([[c2, -s2], [s2, c2]])
    w3 = np.block([[c2, s2], [-s2, c2]])
    angt = 2 * math.pi / TIME * (np.outer(a, b) % TIME)
    tw = np.stack([np.cos(angt), -np.sin(angt)]).astype(np.float32)
    return [np.stack(halves(w)) for w in (w1, w2, w3, w4)] + [tw]


def spectral_call(source, factors, turn):
    w1, w2, w3, w4, tw = spectral_constants()
    vm = pl.BlockSpec(memory_space=pltpu.VMEM)
    return pl.pallas_call(
        spectral_kernel,
        name="spectral",
        out_shape=jax.ShapeDtypeStruct((ZL, 256, 128), F32),
        in_specs=[vm] * 8,
        out_specs=vm,
        scratch_shapes=[pltpu.VMEM((ZL, OUTER, 8, 128), F32)],
        compiler_params=pltpu.CompilerParams(vmem_limit_bytes=32 * 2**20),
        cost_estimate=pl.CostEstimate(flops=3 * 10**9, bytes_accessed=4 * 2**20, transcendentals=0),
    )(source, factors, turn, w1, w2, w3, w4, tw)


def gathered_loss(loss):
    size = lax.axis_size("gz")
    have = loss
    reach = 1
    while reach < size:
        route = [((i + reach) % size, i) for i in range(size)]
        have = jnp.concatenate([have, lax.ppermute(have, "gz", route)], axis=0)
        reach *= 2
    me = lax.axis_index("gz")
    return lax.dynamic_slice_in_dim(jnp.concatenate([have, have], axis=0), size - me, size, 0)


def kerr_tables():
    t = hermite_table()
    t_h, t_l = [part.astype(np.float64) for part in halves(t)]

    def stacked(build):
        return np.concatenate([build(t_h), build(t_h), build(t_l)], axis=1).astype(jnp.bfloat16)

    eye = np.eye(2)

    def sum_q(table):
        return np.einsum("yq,ab->yabq", table, eye).reshape(256, 64)

    def sum_p(table):
        return np.einsum("xkhp,ab->axkhbp", table.reshape(128, 8, 2, 2), eye).reshape(256, 64)

    def sum_y(table):
        return np.einsum("yq,ab->aqyb", table, np.eye(8)).reshape(256, 1024)

    proj = np.stack([sum_y(t_h), sum_y(t_l)]).astype(jnp.bfloat16)
    return stacked(sum_q), stacked(sum_p), proj, np.ascontiguousarray(t.T).astype(np.float32)


def kerr_constants(mode_order, region, chi):
    f2, f3, proj, tt = kerr_tables()
    matches = (region[None, :, :] == jnp.arange(REGIONS, dtype=jnp.int32)[:, None, None]).astype(F32)
    k = 2.0 * jnp.sum(matches * chi[:, None, None], axis=0).T
    index = jnp.arange(MODES, dtype=jnp.int32)
    place = (index[:, None] == mode_order[None, :]).astype(BF)
    back = (mode_order[:, None] == index[None, :]).astype(BF)
    return place, back, f2, f3, proj, tt, k


def on_device(forward, cotangent, mode_order, region, chi, phase, loss):
    me = lax.axis_index("gz")
    both = jnp.concatenate([forward[0], cotangent[0]], axis=0)
    send = both.reshape(4, 32, 32, BLOCK).transpose(2, 0, 1, 3)
    received = lax.all_to_all(send, "ma", split_axis=0, concat_axis=0, tiled=True)
    constants = kerr_constants(mode_order, region, chi)
    source = kerr_call(received, *constants)
    source = source.reshape(256, 8, 128)
    gathered = lax.all_to_all(source, ("gz", "ma"), split_axis=0, concat_axis=0, tiled=True)
    factors = lax.dynamic_slice_in_dim(gathered_loss(loss), me * PER, PER, 1)
    factors = jnp.concatenate([factors, factors], axis=1)
    factors = jnp.broadcast_to(factors[:, None, :, None], (ZL, 1, 8, 128))
    angles = lax.dynamic_slice_in_dim(phase, me * PER, PER, 0)
    angles = angles.reshape(PER, BLOCK, OUTER).transpose(0, 2, 1).reshape(PER * OUTER, BLOCK)
    turn = jnp.stack([jnp.cos(angles), -jnp.sin(angles)])
    result = spectral_call(gathered.reshape(ZL, OUTER, 8, 128), factors, turn)
    result = lax.all_to_all(result, "gz", split_axis=0, concat_axis=0, tiled=True)
    result = result.reshape(8, OUTER, 2, PER, BLOCK).transpose(2, 0, 3, 1, 4)
    return result.reshape(1, 2, 32, TIME)


def solution(mesh):
    in_specs = (
        P("gz", None, "ma", None),
        P("gz", None, "ma", None),
        P(),
        P(),
        P(),
        P("ma", None),
        P("gz", "ma"),
    )
    return jax.shard_map(
        on_device, mesh=mesh, in_specs=in_specs, out_specs=P("gz", None, "ma", None), check_vma=False
    )
```

```python
import math

import jax
import jax.numpy as jnp
import numpy as np
from jax import lax
from jax.experimental import pallas as pl
from jax.experimental.pallas import tpu as pltpu
from jax.sharding import PartitionSpec as P

ORDER = 32
MODES = 1024
GRID = 128
REGIONS = 8
TIME = 4096
BLOCK = 128
OUTER = 32
ZL = 8
PER = 4
BF = jnp.bfloat16
F32 = jnp.float32


def hermite_table():
    step = 20.0 / GRID
    coords = (np.arange(GRID, dtype=np.float64) - (GRID - 1) / 2.0) * step
    columns = [np.exp(-0.5 * coords * coords) * math.pi ** (-0.25)]
    columns.append(math.sqrt(2.0) * coords * columns[0])
    for n in range(2, ORDER):
        columns.append(
            math.sqrt(2.0 / n) * coords * columns[n - 1]
            - math.sqrt((n - 1.0) / n) * columns[n - 2]
        )
    return np.stack(columns, axis=1) * math.sqrt(step)


def halves(array):
    head = array.astype(jnp.bfloat16)
    tail = (array - head.astype(np.float64)).astype(jnp.bfloat16)
    return head, tail


def split(value):
    head = value.astype(BF)
    return head, (value - head.astype(F32)).astype(BF)


def dot(a, b):
    return jnp.dot(a, b, preferred_element_type=F32)


def kerr_kernel(x_ref, place_ref, back_ref, f2_ref, f3_ref, proj_ref, tt_ref, k_ref, o_ref,
                xs, fs, gs, rs, ks, fb):
    def split_in(j, carry):
        rows = pl.ds(pl.multiple_of(j * 32, 32), 32)
        for f in range(4):
            head, tail = split(x_ref[j, f])
            xs[f, rows, 0:128] = head
            xs[f, rows, 128:256] = tail
        return carry

    lax.fori_loop(0, 32, split_in, 0, unroll=4)

    def place(f, carry):
        fs[f] = dot(place_ref[...], xs[f]).astype(BF)
        return carry

    lax.fori_loop(0, 4, place, 0)

    def first(k, carry):
        for pair in range(2):
            got = []
            for h in range(2):
                rows = pl.ds(pl.multiple_of(k * 128 + h * 64, 64), 64)
                a, b = fs[2 * pair, rows, :], fs[2 * pair + 1, rows, :]
                head = jnp.concatenate([a[:, :128], b[:, :128]], axis=1)
                tail = jnp.concatenate([a[:, 128:], b[:, 128:]], axis=1)
                res = dot(f2_ref[...], jnp.concatenate([head, tail, head], axis=0))
                got.append(res.reshape(32, 8, 256))
            low = jnp.concatenate([got[0][:, :4], got[1][:, :4]], axis=1)
            high = jnp.concatenate([got[0][:, 4:], got[1][:, 4:]], axis=1)
            for c in range(2):
                lanes = slice(c * 128, (c + 1) * 128)
                gs[2 * pair + c, :, 0, k] = low[:, :, lanes]
                gs[2 * pair + c, :, 1, k] = high[:, :, lanes]
        return carry

    lax.fori_loop(0, 8, first, 0)

    def grid(v, parity, slot):
        for pair in range(2):
            got = [split(gs[2 * pair + c, v, parity].reshape(64, 128)) for c in range(2)]
            head = jnp.concatenate([got[0][0], got[1][0]], axis=1)
            tail = jnp.concatenate([got[0][1], got[1][1]], axis=1)
            fb[slot, pair] = dot(f3_ref[...], jnp.concatenate([head, tail, head], axis=0))

    def column(v, parity):
        u = 2 * v + parity
        res = []
        for i in range(2):
            xr = slice(i * 128, (i + 1) * 128)
            er, ei = fb[parity, 0, xr, :128], fb[parity, 0, xr, 128:]
            cr, ci = fb[parity, 1, xr, :128], fb[parity, 1, xr, 128:]
            total = er * er + ei * ei
            turn = er * ci - ei * cr
            turn = turn + turn
            gr_h, gr_l = split(total * ci + turn * er)
            gi_h, gi_l = split(turn * ei - total * cr)
            right = jnp.concatenate(
                [jnp.concatenate([gr_h, gi_h], axis=1), jnp.concatenate([gr_l, gi_l], axis=1)], axis=0
            )
            t_h, t_l = split(tt_ref[...] * k_ref[pl.ds(2 * u + i, 1), :])
            left = jnp.concatenate(
                [
                    jnp.concatenate([t_h, t_h], axis=1),
                    jnp.concatenate([t_l, jnp.zeros_like(t_l)], axis=1),
                ],
                axis=0,
            )
            got = dot(left, right)
            res.append(got[:32] + got[32:])
        rows = pl.ds(pl.multiple_of(u * 16, 16), 16)
        for g in range(4):
            both = jnp.concatenate([res[i][g * 8:(g + 1) * 8] for i in range(2)], axis=0)
            head, tail = split(both)
            rs[0, g, rows, :] = head
            rs[1, g, rows, :] = tail

    def columns(v, carry):
        grid(v, 1, 1)
        column(v, 0)
        grid(jnp.minimum(v + 1, GRID // 4 - 1), 0, 0)
        column(v, 1)
        return carry

    grid(0, 0, 0)
    lax.fori_loop(0, GRID // 4, columns, 0, unroll=2)

    def last(g, carry):
        head, tail = rs[0, g], rs[1, g]
        res = dot(proj_ref[0], head) + (dot(proj_ref[0], tail) + dot(proj_ref[1], head))
        rows = pl.ds(pl.multiple_of(g * 256, 256), 256)
        for c in range(2):
            head, tail = split(res[:, c * 128:(c + 1) * 128])
            ks[c, rows, 0:128] = head
            ks[c, rows, 128:256] = tail
        return carry

    lax.fori_loop(0, 4, last, 0)

    def finish(j, carry):
        rows = pl.ds(pl.multiple_of(j * 256, 256), 256)
        for c in range(2):
            res = dot(back_ref[rows, :], ks[c])
            res = res[:, :128] + res[:, 128:]
            for i in range(8):
                value = res[i * 32:(i + 1) * 32] + x_ref[j * 8 + i, 2 + c]
                for g in range(8):
                    o_ref[g, j * 8 + i, c * 4:(c + 1) * 4, :] = value[g * 4:(g + 1) * 4]
        return carry

    lax.fori_loop(0, 4, finish, 0)


def kerr_call(received, *constants):
    vm = pl.BlockSpec(memory_space=pltpu.VMEM)
    return pl.pallas_call(
        kerr_kernel,
        name="kerr",
        out_shape=jax.ShapeDtypeStruct((ZL, 32, 8, 128), F32),
        in_specs=[vm] * (1 + len(constants)),
        out_specs=vm,
        scratch_shapes=[
            pltpu.VMEM((4, MODES, 256), BF),
            pltpu.VMEM((4, MODES, 256), BF),
            pltpu.VMEM((4, 32, 2, 8, 8, 128), F32),
            pltpu.VMEM((2, 4, MODES, 256), BF),
            pltpu.VMEM((2, MODES, 256), BF),
            pltpu.VMEM((2, 2, 256, 256), F32),
        ],
        compiler_params=pltpu.CompilerParams(vmem_limit_bytes=48 * 2**20),
        cost_estimate=pl.CostEstimate(flops=2 * 10**10, bytes_accessed=8 * 2**20, transcendentals=0),
    )(received, *constants)


def three(a_h, a_l, b_h, b_l):
    return dot(a_h, b_h) + (dot(a_h, b_l) + dot(a_l, b_h))


def spectral_kernel(s_ref, l_ref, ph_ref, w1_ref, w2_ref, w3_ref, w4_ref, tw_ref, o_ref, sc):
    for z in range(ZL - 1, -1, -1):
        if z == ZL - 1:
            sc[z] = s_ref[z]
        else:
            sc[z] = s_ref[z] + l_ref[z] * sc[z + 1]
    tw_r = jnp.concatenate([tw_ref[0]] * PER, axis=0)
    tw_i = jnp.concatenate([tw_ref[1]] * PER, axis=0)
    ph_r, ph_i = ph_ref[0], ph_ref[1]

    def pair(j, carry):
        z0 = 2 * j
        a = jnp.concatenate(
            [sc[z0].reshape(256, 128), sc[z0 + 1].reshape(256, 128)], axis=1
        )
        a_h, a_l = split(a)
        first = three(w1_ref[0], w1_ref[1], a_h, a_l)
        outs = []
        for i in range(2):
            re, im = first[:128, i * 128:(i + 1) * 128], first[128:, i * 128:(i + 1) * 128]
            seg = jnp.concatenate([re * tw_r - im * tw_i, re * tw_i + im * tw_r], axis=1)
            s_h, s_l = split(seg)
            spec = three(s_h, s_l, w2_ref[0], w2_ref[1])
            re, im = spec[:, :128], spec[:, 128:]
            spec = jnp.concatenate([re * ph_r - im * ph_i, re * ph_i + im * ph_r], axis=1)
            s_h, s_l = split(spec)
            seg = three(s_h, s_l, w3_ref[0], w3_ref[1])
            re, im = seg[:, :128], seg[:, 128:]
            outs.append(
                jnp.concatenate([re * tw_r + im * tw_i, im * tw_r - re * tw_i], axis=0)
            )
        b_h, b_l = split(jnp.concatenate(outs, axis=1))
        final = three(w4_ref[0], w4_ref[1], b_h, b_l)
        o_ref[z0] = final[:, :128]
        o_ref[z0 + 1] = final[:, 128:]
        return carry

    lax.fori_loop(0, ZL // 2, pair, 0)


def spectral_constants():
    a = np.arange(OUTER)
    ang1 = 2 * math.pi / OUTER * (np.outer(a, a) % OUTER)
    c1, s1 = np.cos(ang1), np.sin(ang1)
    eye = np.eye(PER)
    w1 = np.zeros((2, PER, OUTER, OUTER, 2, PER))
    blocks = {(0, 0): c1, (0, 1): s1, (1, 0): -s1, (1, 1): c1}
    for (co, ci), m in blocks.items():
        w1[co, :, :, :, ci, :] = np.einsum("mn,ka->mkan", eye, m)
    w1 = w1.reshape(256, 256)
    w4 = np.zeros((OUTER, 2, PER, 2, PER, OUTER))
    blocks = {(0, 0): c1, (0, 1): -s1, (1, 0): s1, (1, 1): c1}
    for (co, ci), m in blocks.items():
        w4[:, co, :, ci, :, :] = np.einsum("mn,ka->amnk", eye, m)
    w4 = w4.reshape(256, 256) / TIME
    b = np.arange(BLOCK)
    ang2 = 2 * math.pi / BLOCK * (np.outer(b, b) % BLOCK)
    c2, s2 = np.cos(ang2), np.sin(ang2)
    w2 = np.block([[c2, -s2], [s2, c2]])
    w3 = np.block([[c2, s2], [-s2, c2]])
    angt = 2 * math.pi / TIME * (np.outer(a, b) % TIME)
    tw = np.stack([np.cos(angt), -np.sin(angt)]).astype(np.float32)
    return [np.stack(halves(w)) for w in (w1, w2, w3, w4)] + [tw]


def spectral_call(source, factors, turn):
    w1, w2, w3, w4, tw = spectral_constants()
    vm = pl.BlockSpec(memory_space=pltpu.VMEM)
    return pl.pallas_call(
        spectral_kernel,
        name="spectral",
        out_shape=jax.ShapeDtypeStruct((ZL, 256, 128), F32),
        in_specs=[vm] * 8,
        out_specs=vm,
        scratch_shapes=[pltpu.VMEM((ZL, OUTER, 8, 128), F32)],
        compiler_params=pltpu.CompilerParams(vmem_limit_bytes=32 * 2**20),
        cost_estimate=pl.CostEstimate(flops=3 * 10**9, bytes_accessed=4 * 2**20, transcendentals=0),
    )(source, factors, turn, w1, w2, w3, w4, tw)


def gathered_loss(loss):
    size = lax.axis_size("gz")
    have = loss
    reach = 1
    while reach < size:
        route = [((i + reach) % size, i) for i in range(size)]
        have = jnp.concatenate([have, lax.ppermute(have, "gz", route)], axis=0)
        reach *= 2
    me = lax.axis_index("gz")
    return lax.dynamic_slice_in_dim(jnp.concatenate([have, have], axis=0), size - me, size, 0)


def kerr_tables():
    t = hermite_table()
    t_h, t_l = [part.astype(np.float64) for part in halves(t)]

    def stacked(build):
        return np.concatenate([build(t_h), build(t_h), build(t_l)], axis=1).astype(jnp.bfloat16)

    eye = np.eye(2)

    def sum_q(table):
        return np.einsum("yq,ab->yabq", table, eye).reshape(256, 64)

    def sum_p(table):
        return np.einsum("xkhp,ab->axkhbp", table.reshape(128, 8, 2, 2), eye).reshape(256, 64)

    def sum_y(table):
        return np.einsum("yq,ab->aqyb", table, np.eye(8)).reshape(256, 1024)

    proj = np.stack([sum_y(t_h), sum_y(t_l)]).astype(jnp.bfloat16)
    return stacked(sum_q), stacked(sum_p), proj, np.ascontiguousarray(t.T).astype(np.float32)


def kerr_constants(mode_order, region, chi):
    f2, f3, proj, tt = kerr_tables()
    matches = (region[None, :, :] == jnp.arange(REGIONS, dtype=jnp.int32)[:, None, None]).astype(F32)
    k = 2.0 * jnp.sum(matches * chi[:, None, None], axis=0).T
    index = jnp.arange(MODES, dtype=jnp.int32)
    place = (index[:, None] == mode_order[None, :]).astype(BF)
    back = (mode_order[:, None] == index[None, :]).astype(BF)
    return place, back, f2, f3, proj, tt, k


def on_device(forward, cotangent, mode_order, region, chi, phase, loss):
    me = lax.axis_index("gz")
    both = jnp.concatenate([forward[0], cotangent[0]], axis=0)
    send = both.reshape(4, 32, 32, BLOCK).transpose(2, 0, 1, 3)
    received = lax.all_to_all(send, "ma", split_axis=0, concat_axis=0, tiled=True)
    constants = kerr_constants(mode_order, region, chi)
    source = kerr_call(received, *constants)
    source = source.reshape(256, 8, 128)
    gathered = lax.all_to_all(source, ("gz", "ma"), split_axis=0, concat_axis=0, tiled=True)
    factors = lax.dynamic_slice_in_dim(gathered_loss(loss), me * PER, PER, 1)
    factors = jnp.concatenate([factors, factors], axis=1)
    factors = jnp.broadcast_to(factors[:, None, :, None], (ZL, 1, 8, 128))
    angles = lax.dynamic_slice_in_dim(phase, me * PER, PER, 0)
    angles = angles.reshape(PER, BLOCK, OUTER).transpose(0, 2, 1).reshape(PER * OUTER, BLOCK)
    turn = jnp.stack([jnp.cos(angles), -jnp.sin(angles)])
    result = spectral_call(gathered.reshape(ZL, OUTER, 8, 128), factors, turn)
    result = lax.all_to_all(result, "gz", split_axis=0, concat_axis=0, tiled=True)
    result = result.reshape(8, OUTER, 2, PER, BLOCK).transpose(2, 0, 3, 1, 4)
    return result.reshape(1, 2, 32, TIME)


def solution(mesh):
    in_specs = (
        P("gz", None, "ma", None),
        P("gz", None, "ma", None),
        P(),
        P(),
        P(),
        P("ma", None),
        P("gz", "ma"),
    )
    return jax.shard_map(
        on_device, mesh=mesh, in_specs=in_specs, out_specs=P("gz", None, "ma", None), check_vma=False
    )
```

```python
import math

import jax
import jax.numpy as jnp
import numpy as np
from jax import lax
from jax.experimental import pallas as pl
from jax.experimental.pallas import tpu as pltpu
from jax.sharding import PartitionSpec as P

ORDER = 32
MODES = 1024
GRID = 128
REGIONS = 8
TIME = 4096
BLOCK = 128
OUTER = 32
ZL = 8
PER = 4
BF = jnp.bfloat16
F32 = jnp.float32


def hermite_table():
    step = 20.0 / GRID
    coords = (np.arange(GRID, dtype=np.float64) - (GRID - 1) / 2.0) * step
    columns = [np.exp(-0.5 * coords * coords) * math.pi ** (-0.25)]
    columns.append(math.sqrt(2.0) * coords * columns[0])
    for n in range(2, ORDER):
        columns.append(
            math.sqrt(2.0 / n) * coords * columns[n - 1]
            - math.sqrt((n - 1.0) / n) * columns[n - 2]
        )
    return np.stack(columns, axis=1) * math.sqrt(step)


def halves(array):
    head = array.astype(jnp.bfloat16)
    tail = (array - head.astype(np.float64)).astype(jnp.bfloat16)
    return head, tail


def split(value):
    head = value.astype(BF)
    return head, (value - head.astype(F32)).astype(BF)


def dot(a, b):
    return jnp.dot(a, b, preferred_element_type=F32)


def pack_kernel(f_ref, c_ref, o_ref):
    for j in range(f_ref.shape[3] // 128):
        o_ref[j, 0:2] = f_ref[0, :, :, j * 128:(j + 1) * 128]
        o_ref[j, 2:4] = c_ref[0, :, :, j * 128:(j + 1) * 128]


def pack_call(forward, cotangent):
    steps = 4
    spec = pl.BlockSpec((1, 2, 32, TIME // steps), lambda i: (0, 0, 0, i))
    return pl.pallas_call(
        pack_kernel,
        name="pack",
        grid=(steps,),
        out_shape=jax.ShapeDtypeStruct((32, 4, 32, 128), F32),
        in_specs=[spec, spec],
        out_specs=pl.BlockSpec((32 // steps, 4, 32, 128), lambda i: (i, 0, 0, 0)),
        compiler_params=pltpu.CompilerParams(vmem_limit_bytes=60 * 2**20),
        cost_estimate=pl.CostEstimate(flops=2**20, bytes_accessed=4 * 2**20, transcendentals=0),
    )(forward, cotangent)


def kerr_kernel(x_ref, place_hbm, back_hbm, f2_ref, f3_ref, proj_hbm, tt_ref, k_ref, o_hbm,
                xs, fs, gs, rs, ks, fb, place_ref, back_ref, proj_ref, o_ref, sems, out_sems):
    loads = [
        pltpu.make_async_copy(source, target, sems.at[i])
        for i, (source, target) in enumerate(
            ((place_hbm, place_ref), (proj_hbm, proj_ref), (back_hbm, back_ref))
        )
    ]
    for load in loads:
        load.start()

    def split_in(j, carry):
        rows = pl.ds(pl.multiple_of(j * 32, 32), 32)
        for f in range(4):
            head, tail = split(x_ref[j, f])
            xs[f, rows, 0:128] = head
            xs[f, rows, 128:256] = tail
        return carry

    lax.fori_loop(0, 32, split_in, 0, unroll=4)

    def place(f, carry):
        fs[f] = dot(place_ref[...], xs[f]).astype(BF)
        return carry

    loads[0].wait()
    lax.fori_loop(0, 4, place, 0)

    def first(k, carry):
        for pair in range(2):
            got = []
            for h in range(2):
                rows = pl.ds(pl.multiple_of(k * 128 + h * 64, 64), 64)
                a, b = fs[2 * pair, rows, :], fs[2 * pair + 1, rows, :]
                head = jnp.concatenate([a[:, :128], b[:, :128]], axis=1)
                tail = jnp.concatenate([a[:, 128:], b[:, 128:]], axis=1)
                res = dot(f2_ref[...], jnp.concatenate([head, tail, head], axis=0))
                got.append(res.reshape(32, 8, 256))
            low = jnp.concatenate([got[0][:, :4], got[1][:, :4]], axis=1)
            high = jnp.concatenate([got[0][:, 4:], got[1][:, 4:]], axis=1)
            for c in range(2):
                lanes = slice(c * 128, (c + 1) * 128)
                gs[2 * pair + c, :, 0, k] = low[:, :, lanes]
                gs[2 * pair + c, :, 1, k] = high[:, :, lanes]
        return carry

    lax.fori_loop(0, 8, first, 0, unroll=2)

    def grid(v, parity, slot):
        for pair in range(2):
            got = [split(gs[2 * pair + c, v, parity].reshape(64, 128)) for c in range(2)]
            head = jnp.concatenate([got[0][0], got[1][0]], axis=1)
            tail = jnp.concatenate([got[0][1], got[1][1]], axis=1)
            fb[slot, pair] = dot(f3_ref[...], jnp.concatenate([head, tail, head], axis=0))

    def column(v, parity):
        u = 2 * v + parity
        res = []
        for i in range(2):
            xr = slice(i * 128, (i + 1) * 128)
            er, ei = fb[parity, 0, xr, :128], fb[parity, 0, xr, 128:]
            cr, ci = fb[parity, 1, xr, :128], fb[parity, 1, xr, 128:]
            total = er * er + ei * ei
            turn = er * ci - ei * cr
            turn = turn + turn
            gr_h, gr_l = split(total * ci + turn * er)
            gi_h, gi_l = split(turn * ei - total * cr)
            right = jnp.concatenate(
                [jnp.concatenate([gr_h, gi_h], axis=1), jnp.concatenate([gr_l, gi_l], axis=1)], axis=0
            )
            t_h, t_l = split(tt_ref[...] * k_ref[pl.ds(2 * u + i, 1), :])
            left = jnp.concatenate(
                [
                    jnp.concatenate([t_h, t_h], axis=1),
                    jnp.concatenate([t_l, jnp.zeros_like(t_l)], axis=1),
                ],
                axis=0,
            )
            got = dot(left, right)
            res.append(got[:32] + got[32:])
        rows = pl.ds(pl.multiple_of(u * 16, 16), 16)
        for g in range(4):
            both = jnp.concatenate([res[i][g * 8:(g + 1) * 8] for i in range(2)], axis=0)
            head, tail = split(both)
            rs[0, g, rows, :] = head
            rs[1, g, rows, :] = tail

    def columns(v, carry):
        grid(v, 1, 1)
        column(v, 0)
        grid(jnp.minimum(v + 1, GRID // 4 - 1), 0, 0)
        column(v, 1)
        return carry

    grid(0, 0, 0)
    lax.fori_loop(0, GRID // 4, columns, 0, unroll=2)

    def last(g, carry):
        head, tail = rs[0, g], rs[1, g]
        res = dot(proj_ref[0], head) + (dot(proj_ref[0], tail) + dot(proj_ref[1], head))
        rows = pl.ds(pl.multiple_of(g * 256, 256), 256)
        for c in range(2):
            head, tail = split(res[:, c * 128:(c + 1) * 128])
            ks[c, rows, 0:128] = head
            ks[c, rows, 128:256] = tail
        return carry

    loads[1].wait()
    lax.fori_loop(0, 4, last, 0, unroll=2)

    def store(j):
        part = pl.ds(j * 8, 8)
        return pltpu.make_async_copy(o_ref.at[:, part], o_hbm.at[:, part], out_sems.at[j])

    def finish(j, carry):
        rows = pl.ds(pl.multiple_of(j * 256, 256), 256)
        for c in range(2):
            res = dot(back_ref[rows, :], ks[c])
            res = res[:, :128] + res[:, 128:]
            for i in range(8):
                value = res[i * 32:(i + 1) * 32] + x_ref[j * 8 + i, 2 + c]
                for g in range(8):
                    o_ref[g, j * 8 + i, c * 4:(c + 1) * 4, :] = value[g * 4:(g + 1) * 4]
        store(j).start()
        return carry

    loads[2].wait()
    lax.fori_loop(0, 4, finish, 0)
    for j in range(4):
        store(j).wait()


def kerr_call(received, *constants):
    vm = pl.BlockSpec(memory_space=pltpu.VMEM)
    hbm = pl.BlockSpec(memory_space=pl.ANY)
    return pl.pallas_call(
        kerr_kernel,
        name="kerr",
        out_shape=jax.ShapeDtypeStruct((ZL, 32, 8, 128), F32),
        in_specs=[vm, hbm, hbm, vm, vm, hbm, vm, vm],
        out_specs=hbm,
        scratch_shapes=[
            pltpu.VMEM((4, MODES, 256), BF),
            pltpu.VMEM((4, MODES, 256), BF),
            pltpu.VMEM((4, 32, 2, 8, 8, 128), F32),
            pltpu.VMEM((2, 4, MODES, 256), BF),
            pltpu.VMEM((2, MODES, 256), BF),
            pltpu.VMEM((2, 2, 256, 256), F32),
            pltpu.VMEM((MODES, MODES), BF),
            pltpu.VMEM((MODES, MODES), BF),
            pltpu.VMEM((2, 256, MODES), BF),
            pltpu.VMEM((ZL, 32, 8, 128), F32),
            pltpu.SemaphoreType.DMA((3,)),
            pltpu.SemaphoreType.DMA((4,)),
        ],
        compiler_params=pltpu.CompilerParams(vmem_limit_bytes=54 * 2**20),
        cost_estimate=pl.CostEstimate(flops=2 * 10**10, bytes_accessed=8 * 2**20, transcendentals=0),
    )(received, *constants)


def three(a_h, a_l, b_h, b_l):
    return dot(a_h, b_h) + (dot(a_h, b_l) + dot(a_l, b_h))


def spectral_kernel(s_ref, l_ref, ph_ref, w1_ref, w2_ref, w3_ref, w4_ref, tw_ref, o_ref, sc):
    for z in range(ZL - 1, -1, -1):
        if z == ZL - 1:
            sc[z] = s_ref[z]
        else:
            sc[z] = s_ref[z] + l_ref[z] * sc[z + 1]
    tw_r = jnp.concatenate([tw_ref[0]] * PER, axis=0)
    tw_i = jnp.concatenate([tw_ref[1]] * PER, axis=0)
    ph_r, ph_i = ph_ref[0], ph_ref[1]

    def pair(j, carry):
        z0 = 2 * j
        a = jnp.concatenate(
            [sc[z0].reshape(256, 128), sc[z0 + 1].reshape(256, 128)], axis=1
        )
        a_h, a_l = split(a)
        first = three(w1_ref[0], w1_ref[1], a_h, a_l)
        outs = []
        for i in range(2):
            re, im = first[:128, i * 128:(i + 1) * 128], first[128:, i * 128:(i + 1) * 128]
            seg = jnp.concatenate([re * tw_r - im * tw_i, re * tw_i + im * tw_r], axis=1)
            s_h, s_l = split(seg)
            spec = three(s_h, s_l, w2_ref[0], w2_ref[1])
            re, im = spec[:, :128], spec[:, 128:]
            spec = jnp.concatenate([re * ph_r - im * ph_i, re * ph_i + im * ph_r], axis=1)
            s_h, s_l = split(spec)
            seg = three(s_h, s_l, w3_ref[0], w3_ref[1])
            re, im = seg[:, :128], seg[:, 128:]
            outs.append(
                jnp.concatenate([re * tw_r + im * tw_i, im * tw_r - re * tw_i], axis=0)
            )
        b_h, b_l = split(jnp.concatenate(outs, axis=1))
        final = three(w4_ref[0], w4_ref[1], b_h, b_l)
        o_ref[z0] = final[:, :128]
        o_ref[z0 + 1] = final[:, 128:]
        return carry

    lax.fori_loop(0, ZL // 2, pair, 0)


def spectral_constants():
    a = np.arange(OUTER)
    ang1 = 2 * math.pi / OUTER * (np.outer(a, a) % OUTER)
    c1, s1 = np.cos(ang1), np.sin(ang1)
    eye = np.eye(PER)
    w1 = np.zeros((2, PER, OUTER, OUTER, 2, PER))
    blocks = {(0, 0): c1, (0, 1): s1, (1, 0): -s1, (1, 1): c1}
    for (co, ci), m in blocks.items():
        w1[co, :, :, :, ci, :] = np.einsum("mn,ka->mkan", eye, m)
    w1 = w1.reshape(256, 256)
    w4 = np.zeros((OUTER, 2, PER, 2, PER, OUTER))
    blocks = {(0, 0): c1, (0, 1): -s1, (1, 0): s1, (1, 1): c1}
    for (co, ci), m in blocks.items():
        w4[:, co, :, ci, :, :] = np.einsum("mn,ka->amnk", eye, m)
    w4 = w4.reshape(256, 256) / TIME
    b = np.arange(BLOCK)
    ang2 = 2 * math.pi / BLOCK * (np.outer(b, b) % BLOCK)
    c2, s2 = np.cos(ang2), np.sin(ang2)
    w2 = np.block([[c2, -s2], [s2, c2]])
    w3 = np.block([[c2, s2], [-s2, c2]])
    angt = 2 * math.pi / TIME * (np.outer(a, b) % TIME)
    tw = np.stack([np.cos(angt), -np.sin(angt)]).astype(np.float32)
    return [np.stack(halves(w)) for w in (w1, w2, w3, w4)] + [tw]


def spectral_call(source, factors, turn):
    w1, w2, w3, w4, tw = spectral_constants()
    vm = pl.BlockSpec(memory_space=pltpu.VMEM)
    return pl.pallas_call(
        spectral_kernel,
        name="spectral",
        out_shape=jax.ShapeDtypeStruct((ZL, 256, 128), F32),
        in_specs=[vm] * 8,
        out_specs=vm,
        scratch_shapes=[pltpu.VMEM((ZL, OUTER, 8, 128), F32)],
        compiler_params=pltpu.CompilerParams(vmem_limit_bytes=32 * 2**20),
        cost_estimate=pl.CostEstimate(flops=3 * 10**9, bytes_accessed=4 * 2**20, transcendentals=0),
    )(source, factors, turn, w1, w2, w3, w4, tw)


def gathered_loss(loss):
    size = lax.axis_size("gz")
    have = loss
    reach = 1
    while reach < size:
        route = [((i + reach) % size, i) for i in range(size)]
        have = jnp.concatenate([have, lax.ppermute(have, "gz", route)], axis=0)
        reach *= 2
    me = lax.axis_index("gz")
    return lax.dynamic_slice_in_dim(jnp.concatenate([have, have], axis=0), size - me, size, 0)


def kerr_tables():
    t = hermite_table()
    t_h, t_l = [part.astype(np.float64) for part in halves(t)]

    def stacked(build):
        return np.concatenate([build(t_h), build(t_h), build(t_l)], axis=1).astype(jnp.bfloat16)

    eye = np.eye(2)

    def sum_q(table):
        return np.einsum("yq,ab->yabq", table, eye).reshape(256, 64)

    def sum_p(table):
        return np.einsum("xkhp,ab->axkhbp", table.reshape(128, 8, 2, 2), eye).reshape(256, 64)

    def sum_y(table):
        return np.einsum("yq,ab->aqyb", table, np.eye(8)).reshape(256, 1024)

    proj = np.stack([sum_y(t_h), sum_y(t_l)]).astype(jnp.bfloat16)
    return stacked(sum_q), stacked(sum_p), proj, np.ascontiguousarray(t.T).astype(np.float32)


def kerr_constants(mode_order, region, chi):
    f2, f3, proj, tt = kerr_tables()
    matches = (region[None, :, :] == jnp.arange(REGIONS, dtype=jnp.int32)[:, None, None]).astype(F32)
    k = 2.0 * jnp.sum(matches * chi[:, None, None], axis=0).T
    index = jnp.arange(MODES, dtype=jnp.int32)
    place = (index[:, None] == mode_order[None, :]).astype(BF)
    back = (mode_order[:, None] == index[None, :]).astype(BF)
    return place, back, f2, f3, proj, tt, k


def on_device(forward, cotangent, mode_order, region, chi, phase, loss):
    me = lax.axis_index("gz")
    send = pack_call(forward, cotangent)
    received = lax.all_to_all(send, "ma", split_axis=0, concat_axis=0, tiled=True)
    constants = kerr_constants(mode_order, region, chi)
    source = kerr_call(received, *constants)
    source = source.reshape(256, 8, 128)
    gathered = lax.all_to_all(source, ("gz", "ma"), split_axis=0, concat_axis=0, tiled=True)
    factors = lax.dynamic_slice_in_dim(gathered_loss(loss), me * PER, PER, 1)
    factors = jnp.concatenate([factors, factors], axis=1)
    factors = jnp.broadcast_to(factors[:, None, :, None], (ZL, 1, 8, 128))
    angles = lax.dynamic_slice_in_dim(phase, me * PER, PER, 0)
    angles = angles.reshape(PER, BLOCK, OUTER).transpose(0, 2, 1).reshape(PER * OUTER, BLOCK)
    turn = jnp.stack([jnp.cos(angles), -jnp.sin(angles)])
    result = spectral_call(gathered.reshape(ZL, OUTER, 8, 128), factors, turn)
    result = lax.all_to_all(result, "gz", split_axis=0, concat_axis=0, tiled=True)
    result = result.reshape(8, OUTER, 2, PER, BLOCK).transpose(2, 0, 3, 1, 4)
    return result.reshape(1, 2, 32, TIME)


def solution(mesh):
    in_specs = (
        P("gz", None, "ma", None),
        P("gz", None, "ma", None),
        P(),
        P(),
        P(),
        P("ma", None),
        P("gz", "ma"),
    )
    return jax.shard_map(
        on_device, mesh=mesh, in_specs=in_specs, out_specs=P("gz", None, "ma", None), check_vma=False
    )
```

```python
import functools
import math

import jax
import jax.numpy as jnp
import numpy as np
from jax import lax
from jax.experimental import pallas as pl
from jax.experimental.pallas import tpu as pltpu
from jax.sharding import PartitionSpec as P

ORDER = 32
MODES = 1024
GRID = 128
REGIONS = 8
TIME = 4096
BLOCK = 128
OUTER = 32
ZL = 8
LIMIT = 24 * 2**20
PER = 4
BF = jnp.bfloat16
F32 = jnp.float32


def hermite_table():
    step = 20.0 / GRID
    coords = (np.arange(GRID, dtype=np.float64) - (GRID - 1) / 2.0) * step
    columns = [np.exp(-0.5 * coords * coords) * math.pi ** (-0.25)]
    columns.append(math.sqrt(2.0) * coords * columns[0])
    for n in range(2, ORDER):
        columns.append(
            math.sqrt(2.0 / n) * coords * columns[n - 1]
            - math.sqrt((n - 1.0) / n) * columns[n - 2]
        )
    return np.stack(columns, axis=1) * math.sqrt(step)


def halves(array):
    head = array.astype(jnp.bfloat16)
    tail = (array - head.astype(np.float64)).astype(jnp.bfloat16)
    return head, tail


def split(value):
    head = value.astype(BF)
    return head, (value - head.astype(F32)).astype(BF)


def dot(a, b):
    return jnp.dot(a, b, preferred_element_type=F32)


def swapped(value):
    return pltpu.roll(value, 64, 1)


def pack_kernel(f_ref, c_ref, o_ref, *, half):
    low = lax.broadcasted_iota(jnp.int32, (32, 128), 1) < 64
    for j in range(f_ref.shape[3] // 128):
        lanes = slice(j * 128, (j + 1) * 128)
        for i, ref in enumerate((f_ref, c_ref)):
            re, im = ref[0, 0, :, lanes], ref[0, 1, :, lanes]
            if half:
                o_ref[j, i] = jnp.where(low, swapped(re), im)
            else:
                o_ref[j, i] = jnp.where(low, re, swapped(im))


def pack_call(forward, cotangent, half):
    steps = 4
    spec = pl.BlockSpec((1, 2, 32, TIME // steps), lambda i: (0, 0, 0, i))
    return pl.pallas_call(
        functools.partial(pack_kernel, half=half),
        name="pack",
        grid=(steps,),
        out_shape=jax.ShapeDtypeStruct((32, 2, 32, 128), F32),
        in_specs=[spec, spec],
        out_specs=pl.BlockSpec((32 // steps, 2, 32, 128), lambda i: (i, 0, 0, 0)),
        compiler_params=pltpu.CompilerParams(vmem_limit_bytes=60 * 2**20),
        cost_estimate=pl.CostEstimate(flops=2**20, bytes_accessed=3 * 2**20, transcendentals=0),
    )(forward, cotangent)


def kerr_kernel(x_ref, order_ref, back_hbm, f2_ref, f3_ref, proj_hbm, tt_ref, k_ref, *refs, final):
    if final:
        other_hbm, o_hbm = refs[0], refs[1]
        refs = refs[2:]
    else:
        o_ref = refs[0]
        refs = refs[1:]
    xs, fs, gs, rs, ks, fb, place_ref, back_ref, proj_ref, sems = refs[:10]
    moves = [(proj_hbm, proj_ref), (back_hbm, back_ref)]
    if final:
        other_ref = refs[10]
        moves.append((other_hbm, other_ref))
    loads = [
        pltpu.make_async_copy(source, target, sems.at[i])
        for i, (source, target) in enumerate(moves)
    ]
    for load in loads:
        load.start()

    def one_hot(j, carry):
        rows = pl.ds(pl.multiple_of(j * 32, 32), 32)
        index = lax.broadcasted_iota(jnp.int32, (32, MODES), 0) + j * 32
        place_ref[rows, :] = jnp.where(index == order_ref[...], 1.0, 0.0).astype(BF)
        return carry

    lax.fori_loop(0, 32, one_hot, 0, unroll=2)
    def split_in(j, carry):
        rows = pl.ds(pl.multiple_of(j * 32, 32), 32)
        for f in range(2):
            head, tail = split(x_ref[j, f])
            xs[f, rows, 0:128] = head
            xs[f, rows, 128:256] = tail
        return carry

    lax.fori_loop(0, 32, split_in, 0, unroll=4)

    def place(f, carry):
        fs[f] = dot(place_ref[...], xs[f]).astype(BF)
        return carry

    lax.fori_loop(0, 2, place, 0)

    def first(k, carry):
        got = []
        for h in range(2):
            rows = pl.ds(pl.multiple_of(k * 128 + h * 64, 64), 64)
            a, b = fs[0, rows, :], fs[1, rows, :]
            head = jnp.concatenate([a[:, :128], b[:, :128]], axis=1)
            tail = jnp.concatenate([a[:, 128:], b[:, 128:]], axis=1)
            res = dot(f2_ref[...], jnp.concatenate([head, tail, head], axis=0))
            lanes = []
            for f in range(2):
                v0, v1 = res[:128, f * 128:(f + 1) * 128], res[128:, f * 128:(f + 1) * 128]
                lanes += [jnp.where(low, v0, swapped(v1)), jnp.where(low, swapped(v0), v1)]
            got.append([lane.reshape(16, 8, 128) for lane in lanes])
        for f in range(4):
            a, b = got[0][f], got[1][f]
            lanes = slice(f * 128, (f + 1) * 128)
            gs[:, 0, k, :, lanes] = jnp.concatenate([a[:, :4], b[:, :4]], axis=1)
            gs[:, 1, k, :, lanes] = jnp.concatenate([a[:, 4:], b[:, 4:]], axis=1)
        return carry

    low = lax.broadcasted_iota(jnp.int32, (128, 128), 1) < 64
    lax.fori_loop(0, 8, first, 0, unroll=2)

    def grid(v, parity, slot):
        for pair in range(2):
            head, tail = split(
                gs[v, parity, :, :, pair * 256:(pair + 1) * 256].reshape(64, 256)
            )
            fb[slot, pair] = dot(f3_ref[...], jnp.concatenate([head, tail, head], axis=0))

    def column(v, parity):
        u = 2 * v + parity
        few = low[:32]
        res = ([], [])
        for i in range(2):
            xr = slice(i * 128, (i + 1) * 128)
            er, ei = fb[parity, 0, xr, :128], fb[parity, 0, xr, 128:]
            cr, ci = fb[parity, 1, xr, :128], fb[parity, 1, xr, 128:]
            total = er * er + ei * ei
            turn = er * ci - ei * cr
            turn = turn + turn
            gr_h, gr_l = split(total * ci + turn * er)
            gi_h, gi_l = split(turn * ei - total * cr)
            right = jnp.concatenate(
                [jnp.concatenate([gr_h, gi_h], axis=1), jnp.concatenate([gr_l, gi_l], axis=1)], axis=0
            )
            left = []
            for far in range(2):
                t_h, t_l = split(tt_ref[...] * k_ref[pl.ds(2 * u + i + 64 * far, 1), :])
                left.append(jnp.concatenate([t_h, t_h], axis=1))
                left.append(jnp.concatenate([t_l, jnp.zeros_like(t_l)], axis=1))
            got = dot(jnp.concatenate(left, axis=0), right)
            near, far = got[:32] + got[32:64], got[64:96] + got[96:]
            res[0].append(jnp.where(few, near[:, :128], swapped(near[:, 128:])))
            res[1].append(jnp.where(few, swapped(far[:, :128]), far[:, 128:]))
        for far in range(2):
            rows = pl.ds(pl.multiple_of(u * 16 + 512 * far, 16), 16)
            for g in range(4):
                both = jnp.concatenate([res[far][i][g * 8:(g + 1) * 8] for i in range(2)], axis=0)
                head, tail = split(both)
                lanes = slice(g % 2 * 128, (g % 2 + 1) * 128)
                rs[0, g // 2, rows, lanes] = head
                rs[1, g // 2, rows, lanes] = tail

    def columns(v, carry):
        grid(v, 1, 1)
        column(v, 0)
        grid(jnp.minimum(v + 1, GRID // 8 - 1), 0, 0)
        column(v, 1)
        return carry

    grid(0, 0, 0)
    lax.fori_loop(0, GRID // 8, columns, 0, unroll=2)

    def last(g, carry):
        head, tail = rs[0, g], rs[1, g]
        res = dot(proj_ref[0], head) + (dot(proj_ref[0], tail) + dot(proj_ref[1], head))
        for i in range(2):
            rows = pl.ds(pl.multiple_of(g * 512 + i * 256, 256), 256)
            head, tail = split(res[:, i * 128:(i + 1) * 128])
            ks[rows, 0:128] = head
            ks[rows, 128:256] = tail
        return carry

    loads[0].wait()
    lax.fori_loop(0, 2, last, 0)

    half = lax.broadcasted_iota(jnp.int32, (256, 128), 1) < 64

    def store(j):
        part = pl.ds(j * 8, 8)
        return pltpu.make_async_copy(refs[11].at[:, part], o_hbm.at[:, part], refs[12].at[j])

    def finish(j, carry):
        rows = pl.ds(pl.multiple_of(j * 256, 256), 256)
        res = dot(back_ref[rows, :], ks[...])
        res = res[:, :128] + res[:, 128:]
        cot = jnp.concatenate([x_ref[j * 8 + i, 1] for i in range(8)], axis=0)
        value = cot + res
        if not final:
            o_ref[rows, :] = value
            return carry
        other = other_ref[rows, :]
        parts = (jnp.where(half, other, swapped(value)), jnp.where(half, swapped(other), value))
        for c in range(2):
            for i in range(8):
                for g in range(8):
                    row = i * 32 + g * 4
                    refs[11][g, j * 8 + i, c * 4:(c + 1) * 4, :] = parts[c][row:row + 4]
        store(j).start()
        return carry

    for load in loads[1:]:
        load.wait()
    lax.fori_loop(0, 4, finish, 0)
    if final:
        for j in range(4):
            store(j).wait()


def kerr_call(received, other, *constants):
    vm = pl.BlockSpec(memory_space=pltpu.VMEM)
    hbm = pl.BlockSpec(memory_space=pl.ANY)
    final = other is not None
    shape = (ZL, 32, 8, 128) if final else (MODES, 128)
    scratch = [
        pltpu.VMEM((2, MODES, 256), BF),
        pltpu.VMEM((2, MODES, 256), BF),
        pltpu.VMEM((16, 2, 8, 8, 512), F32),
        pltpu.VMEM((2, 2, MODES, 256), BF),
        pltpu.VMEM((MODES, 256), BF),
        pltpu.VMEM((2, 2, 256, 256), F32),
        pltpu.VMEM((MODES, MODES), BF),
        pltpu.VMEM((MODES, MODES), BF),
        pltpu.VMEM((2, 256, MODES), BF),
        pltpu.SemaphoreType.DMA((3 if final else 2,)),
    ]
    if final:
        scratch += [
            pltpu.VMEM((MODES, 128), F32),
            pltpu.VMEM((ZL, 32, 8, 128), F32),
            pltpu.SemaphoreType.DMA((4,)),
        ]
    return pl.pallas_call(
        functools.partial(kerr_kernel, final=final),
        name="kerr",
        out_shape=jax.ShapeDtypeStruct(shape, F32),
        in_specs=[vm, vm, hbm, vm, vm, hbm, vm, vm] + ([hbm] if final else []),
        out_specs=hbm if final else vm,
        scratch_shapes=scratch,
        compiler_params=pltpu.CompilerParams(vmem_limit_bytes=LIMIT),
        cost_estimate=pl.CostEstimate(flops=10**10, bytes_accessed=8 * 2**20, transcendentals=0),
    )(received, *constants, *([other] if final else []))


def three(a_h, a_l, b_h, b_l):
    return dot(a_h, b_h) + (dot(a_h, b_l) + dot(a_l, b_h))


def spectral_kernel(s_ref, l_ref, ph_ref, w1_ref, w2_ref, w3_ref, w4_ref, tw_ref, o_ref, sc):
    for z in range(ZL - 1, -1, -1):
        if z == ZL - 1:
            sc[z] = s_ref[z]
        else:
            sc[z] = s_ref[z] + l_ref[z] * sc[z + 1]
    tw_r = jnp.concatenate([tw_ref[0]] * PER, axis=0)
    tw_i = jnp.concatenate([tw_ref[1]] * PER, axis=0)
    ph_r, ph_i = ph_ref[0], ph_ref[1]

    def pair(j, carry):
        z0 = 2 * j
        a = jnp.concatenate(
            [sc[z0].reshape(256, 128), sc[z0 + 1].reshape(256, 128)], axis=1
        )
        a_h, a_l = split(a)
        first = three(w1_ref[0], w1_ref[1], a_h, a_l)
        outs = []
        for i in range(2):
            re, im = first[:128, i * 128:(i + 1) * 128], first[128:, i * 128:(i + 1) * 128]
            seg = jnp.concatenate([re * tw_r - im * tw_i, re * tw_i + im * tw_r], axis=1)
            s_h, s_l = split(seg)
            spec = three(s_h, s_l, w2_ref[0], w2_ref[1])
            re, im = spec[:, :128], spec[:, 128:]
            spec = jnp.concatenate([re * ph_r - im * ph_i, re * ph_i + im * ph_r], axis=1)
            s_h, s_l = split(spec)
            seg = three(s_h, s_l, w3_ref[0], w3_ref[1])
            re, im = seg[:, :128], seg[:, 128:]
            outs.append(
                jnp.concatenate([re * tw_r + im * tw_i, im * tw_r - re * tw_i], axis=0)
            )
        b_h, b_l = split(jnp.concatenate(outs, axis=1))
        final = three(w4_ref[0], w4_ref[1], b_h, b_l)
        o_ref[z0] = final[:, :128]
        o_ref[z0 + 1] = final[:, 128:]
        return carry

    lax.fori_loop(0, ZL // 2, pair, 0)


def spectral_constants():
    a = np.arange(OUTER)
    ang1 = 2 * math.pi / OUTER * (np.outer(a, a) % OUTER)
    c1, s1 = np.cos(ang1), np.sin(ang1)
    eye = np.eye(PER)
    w1 = np.zeros((2, PER, OUTER, OUTER, 2, PER))
    blocks = {(0, 0): c1, (0, 1): s1, (1, 0): -s1, (1, 1): c1}
    for (co, ci), m in blocks.items():
        w1[co, :, :, :, ci, :] = np.einsum("mn,ka->mkan", eye, m)
    w1 = w1.reshape(256, 256)
    w4 = np.zeros((OUTER, 2, PER, 2, PER, OUTER))
    blocks = {(0, 0): c1, (0, 1): -s1, (1, 0): s1, (1, 1): c1}
    for (co, ci), m in blocks.items():
        w4[:, co, :, ci, :, :] = np.einsum("mn,ka->amnk", eye, m)
    w4 = w4.reshape(256, 256) / TIME
    b = np.arange(BLOCK)
    ang2 = 2 * math.pi / BLOCK * (np.outer(b, b) % BLOCK)
    c2, s2 = np.cos(ang2), np.sin(ang2)
    w2 = np.block([[c2, -s2], [s2, c2]])
    w3 = np.block([[c2, s2], [-s2, c2]])
    angt = 2 * math.pi / TIME * (np.outer(a, b) % TIME)
    tw = np.stack([np.cos(angt), -np.sin(angt)]).astype(np.float32)
    return [np.stack(halves(w)) for w in (w1, w2, w3, w4)] + [tw]


def spectral_call(source, factors, turn):
    w1, w2, w3, w4, tw = spectral_constants()
    vm = pl.BlockSpec(memory_space=pltpu.VMEM)
    return pl.pallas_call(
        spectral_kernel,
        name="spectral",
        out_shape=jax.ShapeDtypeStruct((ZL, 256, 128), F32),
        in_specs=[vm] * 8,
        out_specs=vm,
        scratch_shapes=[pltpu.VMEM((ZL, OUTER, 8, 128), F32)],
        compiler_params=pltpu.CompilerParams(vmem_limit_bytes=32 * 2**20),
        cost_estimate=pl.CostEstimate(flops=3 * 10**9, bytes_accessed=4 * 2**20, transcendentals=0),
    )(source, factors, turn, w1, w2, w3, w4, tw)


def gathered_loss(loss):
    size = lax.axis_size("gz")
    have = loss
    reach = 1
    while reach < size:
        route = [((i + reach) % size, i) for i in range(size)]
        have = jnp.concatenate([have, lax.ppermute(have, "gz", route)], axis=0)
        reach *= 2
    me = lax.axis_index("gz")
    return lax.dynamic_slice_in_dim(jnp.concatenate([have, have], axis=0), size - me, size, 0)


def kerr_tables():
    t = hermite_table()
    t_h, t_l = [part.astype(np.float64) for part in halves(t)]

    def stacked(build):
        return np.concatenate([build(t_h), build(t_h), build(t_l)], axis=1).astype(jnp.bfloat16)

    eye = np.eye(2)

    def sum_q(table):
        return np.einsum("yq,ab->yabq", table, eye).reshape(256, 64)

    def sum_p(table):
        return np.einsum("xkhp,ab->axkhbp", table.reshape(128, 8, 2, 2), eye).reshape(256, 64)

    def sum_y(table):
        return np.einsum("yq,ab->aqyb", table, np.eye(8)).reshape(256, 1024)

    proj = np.stack([sum_y(t_h), sum_y(t_l)]).astype(jnp.bfloat16)
    return stacked(sum_q), stacked(sum_p), proj, np.ascontiguousarray(t.T).astype(np.float32)


def kerr_constants(mode_order, region, chi):
    f2, f3, proj, tt = kerr_tables()
    matches = (region[None, :, :] == jnp.arange(REGIONS, dtype=jnp.int32)[:, None, None]).astype(F32)
    k = 2.0 * jnp.sum(matches * chi[:, None, None], axis=0).T
    index = jnp.arange(MODES, dtype=jnp.int32)
    back = (mode_order[:, None] == index[None, :]).astype(BF)
    return mode_order[None, :], back, f2, f3, proj, tt, k


def on_device(forward, cotangent, mode_order, region, chi, phase, loss):
    me = lax.axis_index("gz")
    constants = kerr_constants(mode_order, region, chi)
    source = None
    for half in range(2):
        send = pack_call(forward, cotangent, half)
        received = lax.all_to_all(send, "ma", split_axis=0, concat_axis=0, tiled=True)
        source = kerr_call(received, source, *constants)
    source = source.reshape(256, 8, 128)
    gathered = lax.all_to_all(source, ("gz", "ma"), split_axis=0, concat_axis=0, tiled=True)
    factors = lax.dynamic_slice_in_dim(gathered_loss(loss), me * PER, PER, 1)
    factors = jnp.concatenate([factors, factors], axis=1)
    factors = jnp.broadcast_to(factors[:, None, :, None], (ZL, 1, 8, 128))
    angles = lax.dynamic_slice_in_dim(phase, me * PER, PER, 0)
    angles = angles.reshape(PER, BLOCK, OUTER).transpose(0, 2, 1).reshape(PER * OUTER, BLOCK)
    turn = jnp.stack([jnp.cos(angles), -jnp.sin(angles)])
    result = spectral_call(gathered.reshape(ZL, OUTER, 8, 128), factors, turn)
    result = lax.all_to_all(result, "gz", split_axis=0, concat_axis=0, tiled=True)
    result = result.reshape(8, OUTER, 2, PER, BLOCK).transpose(2, 0, 3, 1, 4)
    return result.reshape(1, 2, 32, TIME)


def solution(mesh):
    in_specs = (
        P("gz", None, "ma", None),
        P("gz", None, "ma", None),
        P(),
        P(),
        P(),
        P("ma", None),
        P("gz", "ma"),
    )
    return jax.shard_map(
        on_device, mesh=mesh, in_specs=in_specs, out_specs=P("gz", None, "ma", None), check_vma=False
    )
```

```python
import math

import jax
import jax.numpy as jnp
import numpy as np
from jax import lax
from jax.experimental import pallas as pl
from jax.experimental.pallas import tpu as pltpu
from jax.sharding import PartitionSpec as P

ORDER = 32
MODES = 1024
GRID = 128
REGIONS = 8
TIME = 4096
BLOCK = 128
OUTER = 32
ZL = 8
LIMIT = 48 * 2**20
PER = 4
BF = jnp.bfloat16
F32 = jnp.float32


def hermite_table():
    step = 20.0 / GRID
    coords = (np.arange(GRID, dtype=np.float64) - (GRID - 1) / 2.0) * step
    columns = [np.exp(-0.5 * coords * coords) * math.pi ** (-0.25)]
    columns.append(math.sqrt(2.0) * coords * columns[0])
    for n in range(2, ORDER):
        columns.append(
            math.sqrt(2.0 / n) * coords * columns[n - 1]
            - math.sqrt((n - 1.0) / n) * columns[n - 2]
        )
    return np.stack(columns, axis=1) * math.sqrt(step)


def halves(array):
    head = array.astype(jnp.bfloat16)
    tail = (array - head.astype(np.float64)).astype(jnp.bfloat16)
    return head, tail


def split(value):
    head = value.astype(BF)
    return head, (value - head.astype(F32)).astype(BF)


def dot(a, b):
    return jnp.dot(a, b, preferred_element_type=F32)


def pack_kernel(f_ref, c_ref, o_ref):
    for j in range(f_ref.shape[3] // 128):
        o_ref[j, 0:2] = f_ref[0, :, :, j * 128:(j + 1) * 128]
        o_ref[j, 2:4] = c_ref[0, :, :, j * 128:(j + 1) * 128]


def pack_call(forward, cotangent):
    steps = 4
    spec = pl.BlockSpec((1, 2, 32, TIME // steps), lambda i: (0, 0, 0, i))
    return pl.pallas_call(
        pack_kernel,
        name="pack",
        grid=(steps,),
        out_shape=jax.ShapeDtypeStruct((32, 4, 32, 128), F32),
        in_specs=[spec, spec],
        out_specs=pl.BlockSpec((32 // steps, 4, 32, 128), lambda i: (i, 0, 0, 0)),
        compiler_params=pltpu.CompilerParams(vmem_limit_bytes=60 * 2**20),
        cost_estimate=pl.CostEstimate(flops=2**20, bytes_accessed=4 * 2**20, transcendentals=0),
    )(forward, cotangent)


def kerr_kernel(x_ref, order_ref, back_hbm, f2_ref, f3_ref, proj_hbm, tt_ref, k_ref, o_hbm,
                xs, fs, gs, rs, ks, fb, place_ref, back_ref, proj_ref, o_ref, sems, out_sems):
    loads = [
        pltpu.make_async_copy(source, target, sems.at[i])
        for i, (source, target) in enumerate(
            ((proj_hbm, proj_ref), (back_hbm, back_ref))
        )
    ]
    for load in loads:
        load.start()

    def one_hot(j, carry):
        rows = pl.ds(pl.multiple_of(j * 32, 32), 32)
        index = lax.broadcasted_iota(jnp.int32, (32, MODES), 0) + j * 32
        place_ref[rows, :] = jnp.where(index == order_ref[...], 1.0, 0.0).astype(BF)
        return carry

    lax.fori_loop(0, 32, one_hot, 0, unroll=2)

    def split_in(j, carry):
        rows = pl.ds(pl.multiple_of(j * 32, 32), 32)
        for f in range(4):
            head, tail = split(x_ref[j, f])
            xs[f, rows, 0:128] = head
            xs[f, rows, 128:256] = tail
        return carry

    lax.fori_loop(0, 32, split_in, 0, unroll=4)

    def place(f, carry):
        fs[f] = dot(place_ref[...], xs[f]).astype(BF)
        return carry

    lax.fori_loop(0, 4, place, 0)

    def first(k, carry):
        for pair in range(2):
            got = []
            for h in range(2):
                rows = pl.ds(pl.multiple_of(k * 128 + h * 64, 64), 64)
                a, b = fs[2 * pair, rows, :], fs[2 * pair + 1, rows, :]
                head = jnp.concatenate([a[:, :128], b[:, :128]], axis=1)
                tail = jnp.concatenate([a[:, 128:], b[:, 128:]], axis=1)
                res = dot(f2_ref[...], jnp.concatenate([head, tail, head], axis=0))
                got.append(res.reshape(32, 8, 256))
            low = jnp.concatenate([got[0][:, :4], got[1][:, :4]], axis=1)
            high = jnp.concatenate([got[0][:, 4:], got[1][:, 4:]], axis=1)
            for c in range(2):
                lanes = slice(c * 128, (c + 1) * 128)
                gs[2 * pair + c, :, 0, k] = low[:, :, lanes]
                gs[2 * pair + c, :, 1, k] = high[:, :, lanes]
        return carry

    lax.fori_loop(0, 8, first, 0, unroll=2)

    def grid(v, parity, slot):
        for pair in range(2):
            got = [split(gs[2 * pair + c, v, parity].reshape(64, 128)) for c in range(2)]
            head = jnp.concatenate([got[0][0], got[1][0]], axis=1)
            tail = jnp.concatenate([got[0][1], got[1][1]], axis=1)
            fb[slot, pair] = dot(f3_ref[...], jnp.concatenate([head, tail, head], axis=0))

    def column(v, parity):
        u = 2 * v + parity
        res = []
        for i in range(2):
            xr = slice(i * 128, (i + 1) * 128)
            er, ei = fb[parity, 0, xr, :128], fb[parity, 0, xr, 128:]
            cr, ci = fb[parity, 1, xr, :128], fb[parity, 1, xr, 128:]
            total = er * er + ei * ei
            turn = er * ci - ei * cr
            turn = turn + turn
            gr_h, gr_l = split(total * ci + turn * er)
            gi_h, gi_l = split(turn * ei - total * cr)
            right = jnp.concatenate(
                [jnp.concatenate([gr_h, gi_h], axis=1), jnp.concatenate([gr_l, gi_l], axis=1)], axis=0
            )
            t_h, t_l = split(tt_ref[...] * k_ref[pl.ds(2 * u + i, 1), :])
            left = jnp.concatenate(
                [
                    jnp.concatenate([t_h, t_h], axis=1),
                    jnp.concatenate([t_l, jnp.zeros_like(t_l)], axis=1),
                ],
                axis=0,
            )
            got = dot(left, right)
            res.append(got[:32] + got[32:])
        rows = pl.ds(pl.multiple_of(u * 16, 16), 16)
        for g in range(4):
            both = jnp.concatenate([res[i][g * 8:(g + 1) * 8] for i in range(2)], axis=0)
            head, tail = split(both)
            rs[0, g, rows, :] = head
            rs[1, g, rows, :] = tail

    def columns(v, carry):
        grid(v, 1, 1)
        column(v, 0)
        grid(jnp.minimum(v + 1, GRID // 4 - 1), 0, 0)
        column(v, 1)
        return carry

    grid(0, 0, 0)
    lax.fori_loop(0, GRID // 4, columns, 0, unroll=2)

    def last(g, carry):
        head, tail = rs[0, g], rs[1, g]
        res = dot(proj_ref[0], head) + (dot(proj_ref[0], tail) + dot(proj_ref[1], head))
        rows = pl.ds(pl.multiple_of(g * 256, 256), 256)
        for c in range(2):
            head, tail = split(res[:, c * 128:(c + 1) * 128])
            ks[c, rows, 0:128] = head
            ks[c, rows, 128:256] = tail
        return carry

    loads[0].wait()
    lax.fori_loop(0, 4, last, 0, unroll=2)

    def store(j):
        part = pl.ds(j * 8, 8)
        return pltpu.make_async_copy(o_ref.at[:, part], o_hbm.at[:, part], out_sems.at[j])

    def finish(j, carry):
        rows = pl.ds(pl.multiple_of(j * 256, 256), 256)
        for c in range(2):
            res = dot(back_ref[rows, :], ks[c])
            res = res[:, :128] + res[:, 128:]
            for i in range(8):
                value = res[i * 32:(i + 1) * 32] + x_ref[j * 8 + i, 2 + c]
                for g in range(8):
                    o_ref[g, j * 8 + i, c * 4:(c + 1) * 4, :] = value[g * 4:(g + 1) * 4]
        store(j).start()
        return carry

    loads[1].wait()
    lax.fori_loop(0, 4, finish, 0)
    for j in range(4):
        store(j).wait()


def kerr_call(received, *constants):
    vm = pl.BlockSpec(memory_space=pltpu.VMEM)
    hbm = pl.BlockSpec(memory_space=pl.ANY)
    return pl.pallas_call(
        kerr_kernel,
        name="kerr",
        out_shape=jax.ShapeDtypeStruct((ZL, 32, 8, 128), F32),
        in_specs=[vm, vm, hbm, vm, vm, hbm, vm, vm],
        out_specs=hbm,
        scratch_shapes=[
            pltpu.VMEM((4, MODES, 256), BF),
            pltpu.VMEM((4, MODES, 256), BF),
            pltpu.VMEM((4, 32, 2, 8, 8, 128), F32),
            pltpu.VMEM((2, 4, MODES, 256), BF),
            pltpu.VMEM((2, MODES, 256), BF),
            pltpu.VMEM((2, 2, 256, 256), F32),
            pltpu.VMEM((MODES, MODES), BF),
            pltpu.VMEM((MODES, MODES), BF),
            pltpu.VMEM((2, 256, MODES), BF),
            pltpu.VMEM((ZL, 32, 8, 128), F32),
            pltpu.SemaphoreType.DMA((2,)),
            pltpu.SemaphoreType.DMA((4,)),
        ],
        compiler_params=pltpu.CompilerParams(vmem_limit_bytes=LIMIT),
        cost_estimate=pl.CostEstimate(flops=2 * 10**10, bytes_accessed=8 * 2**20, transcendentals=0),
    )(received, *constants)


def three(a_h, a_l, b_h, b_l):
    return dot(a_h, b_h) + (dot(a_h, b_l) + dot(a_l, b_h))


def spectral_kernel(s_ref, l_ref, ph_ref, w1_ref, w2_ref, w3_ref, w4_ref, tw_ref, o_ref, sc):
    for z in range(ZL - 1, -1, -1):
        if z == ZL - 1:
            sc[z] = s_ref[z]
        else:
            sc[z] = s_ref[z] + l_ref[z] * sc[z + 1]
    tw_r = jnp.concatenate([tw_ref[0]] * PER, axis=0)
    tw_i = jnp.concatenate([tw_ref[1]] * PER, axis=0)
    ph_r, ph_i = ph_ref[0], ph_ref[1]

    def pair(j, carry):
        z0 = 2 * j
        a = jnp.concatenate(
            [sc[z0].reshape(256, 128), sc[z0 + 1].reshape(256, 128)], axis=1
        )
        a_h, a_l = split(a)
        first = three(w1_ref[0], w1_ref[1], a_h, a_l)
        outs = []
        for i in range(2):
            re, im = first[:128, i * 128:(i + 1) * 128], first[128:, i * 128:(i + 1) * 128]
            seg = jnp.concatenate([re * tw_r - im * tw_i, re * tw_i + im * tw_r], axis=1)
            s_h, s_l = split(seg)
            spec = three(s_h, s_l, w2_ref[0], w2_ref[1])
            re, im = spec[:, :128], spec[:, 128:]
            spec = jnp.concatenate([re * ph_r - im * ph_i, re * ph_i + im * ph_r], axis=1)
            s_h, s_l = split(spec)
            seg = three(s_h, s_l, w3_ref[0], w3_ref[1])
            re, im = seg[:, :128], seg[:, 128:]
            outs.append(
                jnp.concatenate([re * tw_r + im * tw_i, im * tw_r - re * tw_i], axis=0)
            )
        b_h, b_l = split(jnp.concatenate(outs, axis=1))
        final = three(w4_ref[0], w4_ref[1], b_h, b_l)
        o_ref[z0] = final[:, :128]
        o_ref[z0 + 1] = final[:, 128:]
        return carry

    lax.fori_loop(0, ZL // 2, pair, 0, unroll=4)


def spectral_constants():
    a = np.arange(OUTER)
    ang1 = 2 * math.pi / OUTER * (np.outer(a, a) % OUTER)
    c1, s1 = np.cos(ang1), np.sin(ang1)
    eye = np.eye(PER)
    w1 = np.zeros((2, PER, OUTER, OUTER, 2, PER))
    blocks = {(0, 0): c1, (0, 1): s1, (1, 0): -s1, (1, 1): c1}
    for (co, ci), m in blocks.items():
        w1[co, :, :, :, ci, :] = np.einsum("mn,ka->mkan", eye, m)
    w1 = w1.reshape(256, 256)
    w4 = np.zeros((OUTER, 2, PER, 2, PER, OUTER))
    blocks = {(0, 0): c1, (0, 1): -s1, (1, 0): s1, (1, 1): c1}
    for (co, ci), m in blocks.items():
        w4[:, co, :, ci, :, :] = np.einsum("mn,ka->amnk", eye, m)
    w4 = w4.reshape(256, 256) / TIME
    b = np.arange(BLOCK)
    ang2 = 2 * math.pi / BLOCK * (np.outer(b, b) % BLOCK)
    c2, s2 = np.cos(ang2), np.sin(ang2)
    w2 = np.block([[c2, -s2], [s2, c2]])
    w3 = np.block([[c2, s2], [-s2, c2]])
    angt = 2 * math.pi / TIME * (np.outer(a, b) % TIME)
    tw = np.stack([np.cos(angt), -np.sin(angt)]).astype(np.float32)
    return [np.stack(halves(w)) for w in (w1, w2, w3, w4)] + [tw]


def spectral_call(source, factors, turn):
    w1, w2, w3, w4, tw = spectral_constants()
    vm = pl.BlockSpec(memory_space=pltpu.VMEM)
    return pl.pallas_call(
        spectral_kernel,
        name="spectral",
        out_shape=jax.ShapeDtypeStruct((ZL, 256, 128), F32),
        in_specs=[vm] * 8,
        out_specs=vm,
        scratch_shapes=[pltpu.VMEM((ZL, OUTER, 8, 128), F32)],
        compiler_params=pltpu.CompilerParams(vmem_limit_bytes=32 * 2**20),
        cost_estimate=pl.CostEstimate(flops=3 * 10**9, bytes_accessed=4 * 2**20, transcendentals=0),
    )(source, factors, turn, w1, w2, w3, w4, tw)


def gathered_loss(loss):
    size = lax.axis_size("gz")
    have = loss
    reach = 1
    while reach < size:
        route = [((i + reach) % size, i) for i in range(size)]
        have = jnp.concatenate([have, lax.ppermute(have, "gz", route)], axis=0)
        reach *= 2
    me = lax.axis_index("gz")
    return lax.dynamic_slice_in_dim(jnp.concatenate([have, have], axis=0), size - me, size, 0)


def kerr_tables():
    t = hermite_table()
    t_h, t_l = [part.astype(np.float64) for part in halves(t)]

    def stacked(build):
        return np.concatenate([build(t_h), build(t_h), build(t_l)], axis=1).astype(jnp.bfloat16)

    eye = np.eye(2)

    def sum_q(table):
        return np.einsum("yq,ab->yabq", table, eye).reshape(256, 64)

    def sum_p(table):
        return np.einsum("xkhp,ab->axkhbp", table.reshape(128, 8, 2, 2), eye).reshape(256, 64)

    def sum_y(table):
        return np.einsum("yq,ab->aqyb", table, np.eye(8)).reshape(256, 1024)

    proj = np.stack([sum_y(t_h), sum_y(t_l)]).astype(jnp.bfloat16)
    return stacked(sum_q), stacked(sum_p), proj, np.ascontiguousarray(t.T).astype(np.float32)


def kerr_constants(mode_order, region, chi):
    f2, f3, proj, tt = kerr_tables()
    matches = (region[None, :, :] == jnp.arange(REGIONS, dtype=jnp.int32)[:, None, None]).astype(F32)
    k = 2.0 * jnp.sum(matches * chi[:, None, None], axis=0).T
    index = jnp.arange(MODES, dtype=jnp.int32)
    back = (mode_order[:, None] == index[None, :]).astype(BF)
    return mode_order[None, :], back, f2, f3, proj, tt, k


def on_device(forward, cotangent, mode_order, region, chi, phase, loss):
    me = lax.axis_index("gz")
    send = pack_call(forward, cotangent)
    received = lax.all_to_all(send, "ma", split_axis=0, concat_axis=0, tiled=True)
    constants = kerr_constants(mode_order, region, chi)
    source = kerr_call(received, *constants)
    source = source.reshape(256, 8, 128)
    gathered = lax.all_to_all(source, ("gz", "ma"), split_axis=0, concat_axis=0, tiled=True)
    factors = lax.dynamic_slice_in_dim(gathered_loss(loss), me * PER, PER, 1)
    factors = jnp.concatenate([factors, factors], axis=1)
    factors = jnp.broadcast_to(factors[:, None, :, None], (ZL, 1, 8, 128))
    angles = lax.dynamic_slice_in_dim(phase, me * PER, PER, 0)
    angles = angles.reshape(PER, BLOCK, OUTER).transpose(0, 2, 1).reshape(PER * OUTER, BLOCK)
    turn = jnp.stack([jnp.cos(angles), -jnp.sin(angles)])
    result = spectral_call(gathered.reshape(ZL, OUTER, 8, 128), factors, turn)
    result = lax.all_to_all(result, "gz", split_axis=0, concat_axis=0, tiled=True)
    result = result.reshape(8, OUTER, 2, PER, BLOCK).transpose(2, 0, 3, 1, 4)
    return result.reshape(1, 2, 32, TIME)


def solution(mesh):
    in_specs = (
        P("gz", None, "ma", None),
        P("gz", None, "ma", None),
        P(),
        P(),
        P(),
        P("ma", None),
        P("gz", "ma"),
    )
    return jax.shard_map(
        on_device, mesh=mesh, in_specs=in_specs, out_specs=P("gz", None, "ma", None), check_vma=False
    )
```

```python
import math

import jax
import jax.numpy as jnp
import numpy as np
from jax import lax
from jax.experimental import pallas as pl
from jax.experimental.pallas import tpu as pltpu
from jax.sharding import PartitionSpec as P

ORDER = 32
MODES = 1024
GRID = 128
REGIONS = 8
TIME = 4096
BLOCK = 128
OUTER = 32
ZL = 8
LIMIT = 48 * 2**20
PER = 4
BF = jnp.bfloat16
F32 = jnp.float32


def hermite_table():
    step = 20.0 / GRID
    coords = (np.arange(GRID, dtype=np.float64) - (GRID - 1) / 2.0) * step
    columns = [np.exp(-0.5 * coords * coords) * math.pi ** (-0.25)]
    columns.append(math.sqrt(2.0) * coords * columns[0])
    for n in range(2, ORDER):
        columns.append(
            math.sqrt(2.0 / n) * coords * columns[n - 1]
            - math.sqrt((n - 1.0) / n) * columns[n - 2]
        )
    return np.stack(columns, axis=1) * math.sqrt(step)


def halves(array):
    head = array.astype(jnp.bfloat16)
    tail = (array - head.astype(np.float64)).astype(jnp.bfloat16)
    return head, tail


def split(value):
    head = value.astype(BF)
    return head, (value - head.astype(F32)).astype(BF)


def dot(a, b):
    return jnp.dot(a, b, preferred_element_type=F32)


def pack_kernel(f_ref, c_ref, o_ref):
    for j in range(f_ref.shape[3] // 128):
        o_ref[j, 0:2] = f_ref[0, :, :, j * 128:(j + 1) * 128]
        o_ref[j, 2:4] = c_ref[0, :, :, j * 128:(j + 1) * 128]


def pack_call(forward, cotangent):
    steps = 2
    spec = pl.BlockSpec((1, 2, 32, TIME // steps), lambda i: (0, 0, 0, i))
    return pl.pallas_call(
        pack_kernel,
        name="pack",
        grid=(steps,),
        out_shape=jax.ShapeDtypeStruct((32, 4, 32, 128), F32),
        in_specs=[spec, spec],
        out_specs=pl.BlockSpec((32 // steps, 4, 32, 128), lambda i: (i, 0, 0, 0)),
        compiler_params=pltpu.CompilerParams(vmem_limit_bytes=60 * 2**20),
        cost_estimate=pl.CostEstimate(flops=2**20, bytes_accessed=4 * 2**20, transcendentals=0),
    )(forward, cotangent)


def kerr_kernel(x_ref, order_ref, back_hbm, f2_ref, f3_ref, proj_hbm, tt_ref, k_ref, o_hbm,
                xs, fs, gs, rs, ks, fb, place_ref, back_ref, proj_ref, o_ref, sems, out_sems):
    loads = [
        pltpu.make_async_copy(source, target, sems.at[i])
        for i, (source, target) in enumerate(
            ((proj_hbm, proj_ref), (back_hbm, back_ref))
        )
    ]
    for load in loads:
        load.start()

    def one_hot(j, carry):
        rows = pl.ds(pl.multiple_of(j * 32, 32), 32)
        index = lax.broadcasted_iota(jnp.int32, (32, MODES), 0) + j * 32
        place_ref[rows, :] = jnp.where(index == order_ref[...], 1.0, 0.0).astype(BF)
        return carry

    lax.fori_loop(0, 32, one_hot, 0, unroll=2)

    def split_in(j, carry):
        rows = pl.ds(pl.multiple_of(j * 32, 32), 32)
        for f in range(4):
            head, tail = split(x_ref[j, f])
            xs[f, rows, 0:128] = head
            xs[f, rows, 128:256] = tail
        return carry

    lax.fori_loop(0, 32, split_in, 0, unroll=4)

    def place(f, carry):
        fs[f] = dot(place_ref[...], xs[f]).astype(BF)
        return carry

    lax.fori_loop(0, 4, place, 0, unroll=2)

    def first(k, carry):
        for pair in range(2):
            got = []
            for h in range(2):
                rows = pl.ds(pl.multiple_of(k * 128 + h * 64, 64), 64)
                a, b = fs[2 * pair, rows, :], fs[2 * pair + 1, rows, :]
                head = jnp.concatenate([a[:, :128], b[:, :128]], axis=1)
                tail = jnp.concatenate([a[:, 128:], b[:, 128:]], axis=1)
                res = dot(f2_ref[...], jnp.concatenate([head, tail, head], axis=0))
                got.append(res.reshape(32, 8, 256))
            low = jnp.concatenate([got[0][:, :4], got[1][:, :4]], axis=1)
            high = jnp.concatenate([got[0][:, 4:], got[1][:, 4:]], axis=1)
            for c in range(2):
                lanes = slice(c * 128, (c + 1) * 128)
                gs[2 * pair + c, :, 0, k] = low[:, :, lanes]
                gs[2 * pair + c, :, 1, k] = high[:, :, lanes]
        return carry

    lax.fori_loop(0, 8, first, 0, unroll=2)

    def grid(v, parity, slot):
        for pair in range(2):
            got = [split(gs[2 * pair + c, v, parity].reshape(64, 128)) for c in range(2)]
            head = jnp.concatenate([got[0][0], got[1][0]], axis=1)
            tail = jnp.concatenate([got[0][1], got[1][1]], axis=1)
            fb[slot, pair] = dot(f3_ref[...], jnp.concatenate([head, tail, head], axis=0))

    def column(v, parity):
        u = 2 * v + parity
        res = []
        for i in range(2):
            xr = slice(i * 128, (i + 1) * 128)
            er, ei = fb[parity, 0, xr, :128], fb[parity, 0, xr, 128:]
            cr, ci = fb[parity, 1, xr, :128], fb[parity, 1, xr, 128:]
            total = er * er + ei * ei
            turn = er * ci - ei * cr
            turn = turn + turn
            gr_h, gr_l = split(total * ci + turn * er)
            gi_h, gi_l = split(turn * ei - total * cr)
            right = jnp.concatenate(
                [jnp.concatenate([gr_h, gi_h], axis=1), jnp.concatenate([gr_l, gi_l], axis=1)], axis=0
            )
            t_h, t_l = split(tt_ref[...] * k_ref[pl.ds(2 * u + i, 1), :])
            left = jnp.concatenate(
                [
                    jnp.concatenate([t_h, t_h], axis=1),
                    jnp.concatenate([t_l, jnp.zeros_like(t_l)], axis=1),
                ],
                axis=0,
            )
            got = dot(left, right)
            res.append(got[:32] + got[32:])
        rows = pl.ds(pl.multiple_of(u * 16, 16), 16)
        for g in range(4):
            both = jnp.concatenate([res[i][g * 8:(g + 1) * 8] for i in range(2)], axis=0)
            head, tail = split(both)
            rs[0, g, rows, :] = head
            rs[1, g, rows, :] = tail

    def columns(v, carry):
        grid(v, 1, 1)
        column(v, 0)
        grid(jnp.minimum(v + 1, GRID // 4 - 1), 0, 0)
        column(v, 1)
        return carry

    grid(0, 0, 0)
    lax.fori_loop(0, GRID // 4, columns, 0, unroll=4)

    def last(g, carry):
        head, tail = rs[0, g], rs[1, g]
        res = dot(proj_ref[0], head) + (dot(proj_ref[0], tail) + dot(proj_ref[1], head))
        rows = pl.ds(pl.multiple_of(g * 256, 256), 256)
        for c in range(2):
            head, tail = split(res[:, c * 128:(c + 1) * 128])
            ks[c, rows, 0:128] = head
            ks[c, rows, 128:256] = tail
        return carry

    loads[0].wait()
    lax.fori_loop(0, 4, last, 0, unroll=2)

    def store(j):
        part = pl.ds(j * 8, 8)
        return pltpu.make_async_copy(o_ref.at[:, part], o_hbm.at[:, part], out_sems.at[j])

    def finish(j, carry):
        rows = pl.ds(pl.multiple_of(j * 256, 256), 256)
        for c in range(2):
            res = dot(back_ref[rows, :], ks[c])
            res = res[:, :128] + res[:, 128:]
            for i in range(8):
                value = res[i * 32:(i + 1) * 32] + x_ref[j * 8 + i, 2 + c]
                for g in range(8):
                    o_ref[g, j * 8 + i, c * 4:(c + 1) * 4, :] = value[g * 4:(g + 1) * 4]
        store(j).start()
        return carry

    loads[1].wait()
    lax.fori_loop(0, 4, finish, 0, unroll=2)
    for j in range(4):
        store(j).wait()


def kerr_call(received, *constants):
    vm = pl.BlockSpec(memory_space=pltpu.VMEM)
    hbm = pl.BlockSpec(memory_space=pl.ANY)
    return pl.pallas_call(
        kerr_kernel,
        name="kerr",
        out_shape=jax.ShapeDtypeStruct((ZL, 32, 8, 128), F32),
        in_specs=[vm, vm, hbm, vm, vm, hbm, vm, vm],
        out_specs=hbm,
        scratch_shapes=[
            pltpu.VMEM((4, MODES, 256), BF),
            pltpu.VMEM((4, MODES, 256), BF),
            pltpu.VMEM((4, 32, 2, 8, 8, 128), F32),
            pltpu.VMEM((2, 4, MODES, 256), BF),
            pltpu.VMEM((2, MODES, 256), BF),
            pltpu.VMEM((2, 2, 256, 256), F32),
            pltpu.VMEM((MODES, MODES), BF),
            pltpu.VMEM((MODES, MODES), BF),
            pltpu.VMEM((2, 256, MODES), BF),
            pltpu.VMEM((ZL, 32, 8, 128), F32),
            pltpu.SemaphoreType.DMA((2,)),
            pltpu.SemaphoreType.DMA((4,)),
        ],
        compiler_params=pltpu.CompilerParams(vmem_limit_bytes=LIMIT),
        cost_estimate=pl.CostEstimate(flops=2 * 10**10, bytes_accessed=8 * 2**20, transcendentals=0),
    )(received, *constants)


def three(a_h, a_l, b_h, b_l):
    return dot(a_h, b_h) + (dot(a_h, b_l) + dot(a_l, b_h))


def spectral_kernel(s_ref, l_ref, ph_ref, w1_ref, w2_ref, w3_ref, w4_ref, tw_ref, o_ref, sc):
    for z in range(ZL - 1, -1, -1):
        if z == ZL - 1:
            sc[z] = s_ref[z]
        else:
            sc[z] = s_ref[z] + l_ref[z] * sc[z + 1]
    tw_r = jnp.concatenate([tw_ref[0]] * PER, axis=0)
    tw_i = jnp.concatenate([tw_ref[1]] * PER, axis=0)
    ph_r, ph_i = ph_ref[0], ph_ref[1]

    def pair(j, carry):
        z0 = 2 * j
        a = jnp.concatenate(
            [sc[z0].reshape(256, 128), sc[z0 + 1].reshape(256, 128)], axis=1
        )
        a_h, a_l = split(a)
        first = three(w1_ref[0], w1_ref[1], a_h, a_l)
        outs = []
        for i in range(2):
            re, im = first[:128, i * 128:(i + 1) * 128], first[128:, i * 128:(i + 1) * 128]
            seg = jnp.concatenate([re * tw_r - im * tw_i, re * tw_i + im * tw_r], axis=1)
            s_h, s_l = split(seg)
            spec = three(s_h, s_l, w2_ref[0], w2_ref[1])
            re, im = spec[:, :128], spec[:, 128:]
            spec = jnp.concatenate([re * ph_r - im * ph_i, re * ph_i + im * ph_r], axis=1)
            s_h, s_l = split(spec)
            seg = three(s_h, s_l, w3_ref[0], w3_ref[1])
            re, im = seg[:, :128], seg[:, 128:]
            outs.append(
                jnp.concatenate([re * tw_r + im * tw_i, im * tw_r - re * tw_i], axis=0)
            )
        b_h, b_l = split(jnp.concatenate(outs, axis=1))
        final = three(w4_ref[0], w4_ref[1], b_h, b_l)
        o_ref[z0] = final[:, :128]
        o_ref[z0 + 1] = final[:, 128:]
        return carry

    lax.fori_loop(0, ZL // 2, pair, 0, unroll=4)


def spectral_constants():
    a = np.arange(OUTER)
    ang1 = 2 * math.pi / OUTER * (np.outer(a, a) % OUTER)
    c1, s1 = np.cos(ang1), np.sin(ang1)
    eye = np.eye(PER)
    w1 = np.zeros((2, PER, OUTER, OUTER, 2, PER))
    blocks = {(0, 0): c1, (0, 1): s1, (1, 0): -s1, (1, 1): c1}
    for (co, ci), m in blocks.items():
        w1[co, :, :, :, ci, :] = np.einsum("mn,ka->mkan", eye, m)
    w1 = w1.reshape(256, 256)
    w4 = np.zeros((OUTER, 2, PER, 2, PER, OUTER))
    blocks = {(0, 0): c1, (0, 1): -s1, (1, 0): s1, (1, 1): c1}
    for (co, ci), m in blocks.items():
        w4[:, co, :, ci, :, :] = np.einsum("mn,ka->amnk", eye, m)
    w4 = w4.reshape(256, 256) / TIME
    b = np.arange(BLOCK)
    ang2 = 2 * math.pi / BLOCK * (np.outer(b, b) % BLOCK)
    c2, s2 = np.cos(ang2), np.sin(ang2)
    w2 = np.block([[c2, -s2], [s2, c2]])
    w3 = np.block([[c2, s2], [-s2, c2]])
    angt = 2 * math.pi / TIME * (np.outer(a, b) % TIME)
    tw = np.stack([np.cos(angt), -np.sin(angt)]).astype(np.float32)
    return [np.stack(halves(w)) for w in (w1, w2, w3, w4)] + [tw]


def spectral_call(source, factors, turn):
    w1, w2, w3, w4, tw = spectral_constants()
    vm = pl.BlockSpec(memory_space=pltpu.VMEM)
    return pl.pallas_call(
        spectral_kernel,
        name="spectral",
        out_shape=jax.ShapeDtypeStruct((ZL, 256, 128), F32),
        in_specs=[vm] * 8,
        out_specs=vm,
        scratch_shapes=[pltpu.VMEM((ZL, OUTER, 8, 128), F32)],
        compiler_params=pltpu.CompilerParams(vmem_limit_bytes=32 * 2**20),
        cost_estimate=pl.CostEstimate(flops=3 * 10**9, bytes_accessed=4 * 2**20, transcendentals=0),
    )(source, factors, turn, w1, w2, w3, w4, tw)


def gathered_loss(loss):
    size = lax.axis_size("gz")
    have = loss
    reach = 1
    while reach < size:
        route = [((i + reach) % size, i) for i in range(size)]
        have = jnp.concatenate([have, lax.ppermute(have, "gz", route)], axis=0)
        reach *= 2
    me = lax.axis_index("gz")
    return lax.dynamic_slice_in_dim(jnp.concatenate([have, have], axis=0), size - me, size, 0)


def kerr_tables():
    t = hermite_table()
    t_h, t_l = [part.astype(np.float64) for part in halves(t)]

    def stacked(build):
        return np.concatenate([build(t_h), build(t_h), build(t_l)], axis=1).astype(jnp.bfloat16)

    eye = np.eye(2)

    def sum_q(table):
        return np.einsum("yq,ab->yabq", table, eye).reshape(256, 64)

    def sum_p(table):
        return np.einsum("xkhp,ab->axkhbp", table.reshape(128, 8, 2, 2), eye).reshape(256, 64)

    def sum_y(table):
        return np.einsum("yq,ab->aqyb", table, np.eye(8)).reshape(256, 1024)

    proj = np.stack([sum_y(t_h), sum_y(t_l)]).astype(jnp.bfloat16)
    return stacked(sum_q), stacked(sum_p), proj, np.ascontiguousarray(t.T).astype(np.float32)


def kerr_constants(mode_order, region, chi):
    f2, f3, proj, tt = kerr_tables()
    matches = (region[None, :, :] == jnp.arange(REGIONS, dtype=jnp.int32)[:, None, None]).astype(F32)
    k = 2.0 * jnp.sum(matches * chi[:, None, None], axis=0).T
    index = jnp.arange(MODES, dtype=jnp.int32)
    back = (mode_order[:, None] == index[None, :]).astype(BF)
    return mode_order[None, :], back, f2, f3, proj, tt, k


def on_device(forward, cotangent, mode_order, region, chi, phase, loss):
    me = lax.axis_index("gz")
    send = pack_call(forward, cotangent)
    received = lax.all_to_all(send, "ma", split_axis=0, concat_axis=0, tiled=True)
    constants = kerr_constants(mode_order, region, chi)
    source = kerr_call(received, *constants)
    source = source.reshape(256, 8, 128)
    gathered = lax.all_to_all(source, ("gz", "ma"), split_axis=0, concat_axis=0, tiled=True)
    factors = lax.dynamic_slice_in_dim(gathered_loss(loss), me * PER, PER, 1)
    factors = jnp.concatenate([factors, factors], axis=1)
    factors = jnp.broadcast_to(factors[:, None, :, None], (ZL, 1, 8, 128))
    angles = lax.dynamic_slice_in_dim(phase, me * PER, PER, 0)
    angles = angles.reshape(PER, BLOCK, OUTER).transpose(0, 2, 1).reshape(PER * OUTER, BLOCK)
    turn = jnp.stack([jnp.cos(angles), -jnp.sin(angles)])
    result = spectral_call(gathered.reshape(ZL, OUTER, 8, 128), factors, turn)
    result = lax.all_to_all(result, "gz", split_axis=0, concat_axis=0, tiled=True)
    result = result.reshape(8, OUTER, 2, PER, BLOCK).transpose(2, 0, 3, 1, 4)
    return result.reshape(1, 2, 32, TIME)


def solution(mesh):
    in_specs = (
        P("gz", None, "ma", None),
        P("gz", None, "ma", None),
        P(),
        P(),
        P(),
        P("ma", None),
        P("gz", "ma"),
    )
    return jax.shard_map(
        on_device, mesh=mesh, in_specs=in_specs, out_specs=P("gz", None, "ma", None), check_vma=False
    )
```

```python
import math

import jax
import jax.numpy as jnp
import numpy as np
from jax import lax
from jax.experimental import pallas as pl
from jax.experimental.pallas import tpu as pltpu
from jax.sharding import PartitionSpec as P

ORDER = 32
MODES = 1024
GRID = 128
REGIONS = 8
TIME = 4096
BLOCK = 128
OUTER = 32
ZL = 8
LIMIT = 50 * 2**20
PER = 4
BF = jnp.bfloat16
F32 = jnp.float32


def hermite_table():
    step = 20.0 / GRID
    coords = (np.arange(GRID, dtype=np.float64) - (GRID - 1) / 2.0) * step
    columns = [np.exp(-0.5 * coords * coords) * math.pi ** (-0.25)]
    columns.append(math.sqrt(2.0) * coords * columns[0])
    for n in range(2, ORDER):
        columns.append(
            math.sqrt(2.0 / n) * coords * columns[n - 1]
            - math.sqrt((n - 1.0) / n) * columns[n - 2]
        )
    return np.stack(columns, axis=1) * math.sqrt(step)


def halves(array):
    head = array.astype(jnp.bfloat16)
    tail = (array - head.astype(np.float64)).astype(jnp.bfloat16)
    return head, tail


def split(value):
    head = value.astype(BF)
    return head, (value - head.astype(F32)).astype(BF)


def dot(a, b):
    return jnp.dot(a, b, preferred_element_type=F32)


def pack_kernel(f_ref, c_ref, o_ref):
    for j in range(f_ref.shape[3] // 128):
        o_ref[j, 0:2] = f_ref[0, :, :, j * 128:(j + 1) * 128]
        o_ref[j, 2:4] = c_ref[0, :, :, j * 128:(j + 1) * 128]


def pack_call(forward, cotangent):
    steps = 2
    spec = pl.BlockSpec((1, 2, 32, TIME // steps), lambda i: (0, 0, 0, i))
    return pl.pallas_call(
        pack_kernel,
        name="pack",
        grid=(steps,),
        out_shape=jax.ShapeDtypeStruct((32, 4, 32, 128), F32),
        in_specs=[spec, spec],
        out_specs=pl.BlockSpec((32 // steps, 4, 32, 128), lambda i: (i, 0, 0, 0)),
        compiler_params=pltpu.CompilerParams(vmem_limit_bytes=60 * 2**20),
        cost_estimate=pl.CostEstimate(flops=2**20, bytes_accessed=4 * 2**20, transcendentals=0),
    )(forward, cotangent)


def kerr_kernel(x_ref, order_ref, back_hbm, f2_ref, f3_ref, proj_hbm, tt_ref, k_ref, o_hbm,
                xs, fs, gs, rs, ks, fb, place_ref, back_ref, proj_ref, o_ref, sems, out_sems):
    loads = [
        pltpu.make_async_copy(source, target, sems.at[i])
        for i, (source, target) in enumerate(
            ((proj_hbm, proj_ref), (back_hbm, back_ref))
        )
    ]
    for load in loads:
        load.start()

    def one_hot(j, carry):
        rows = pl.ds(pl.multiple_of(j * 32, 32), 32)
        index = lax.broadcasted_iota(jnp.int32, (32, MODES), 0) + j * 32
        place_ref[rows, :] = jnp.where(index == order_ref[...], 1.0, 0.0).astype(BF)
        return carry

    lax.fori_loop(0, 32, one_hot, 0, unroll=2)

    def split_in(j, carry):
        rows = pl.ds(pl.multiple_of(j * 32, 32), 32)
        for f in range(4):
            head, tail = split(x_ref[j, f])
            xs[f, rows, 0:128] = head
            xs[f, rows, 128:256] = tail
        return carry

    lax.fori_loop(0, 32, split_in, 0, unroll=4)

    def place(f, carry):
        fs[f] = dot(place_ref[...], xs[f]).astype(BF)
        return carry

    lax.fori_loop(0, 4, place, 0, unroll=2)

    def first(k, carry):
        for pair in range(2):
            got = []
            for h in range(2):
                rows = pl.ds(pl.multiple_of(k * 128 + h * 64, 64), 64)
                a, b = fs[2 * pair, rows, :], fs[2 * pair + 1, rows, :]
                head = jnp.concatenate([a[:, :128], b[:, :128]], axis=1)
                tail = jnp.concatenate([a[:, 128:], b[:, 128:]], axis=1)
                res = dot(f2_ref[...], jnp.concatenate([head, tail, head], axis=0))
                got.append(res.reshape(32, 8, 256))
            low = jnp.concatenate([got[0][:, :4], got[1][:, :4]], axis=1)
            high = jnp.concatenate([got[0][:, 4:], got[1][:, 4:]], axis=1)
            for c in range(2):
                lanes = slice(c * 128, (c + 1) * 128)
                gs[2 * pair + c, :, 0, k] = low[:, :, lanes]
                gs[2 * pair + c, :, 1, k] = high[:, :, lanes]
        return carry

    lax.fori_loop(0, 8, first, 0, unroll=2)

    def grid(v, parity, slot):
        for pair in range(2):
            got = [split(gs[2 * pair + c, v, parity].reshape(64, 128)) for c in range(2)]
            head = jnp.concatenate([got[0][0], got[1][0]], axis=1)
            tail = jnp.concatenate([got[0][1], got[1][1]], axis=1)
            fb[slot, pair] = dot(f3_ref[...], jnp.concatenate([head, tail, head], axis=0))

    def column(v, parity):
        u = 2 * v + parity
        res = []
        for i in range(2):
            xr = slice(i * 128, (i + 1) * 128)
            er, ei = fb[parity, 0, xr, :128], fb[parity, 0, xr, 128:]
            cr, ci = fb[parity, 1, xr, :128], fb[parity, 1, xr, 128:]
            total = er * er + ei * ei
            turn = er * ci - ei * cr
            turn = turn + turn
            gr_h, gr_l = split(total * ci + turn * er)
            gi_h, gi_l = split(turn * ei - total * cr)
            right = jnp.concatenate(
                [jnp.concatenate([gr_h, gi_h], axis=1), jnp.concatenate([gr_l, gi_l], axis=1)], axis=0
            )
            t_h, t_l = split(tt_ref[...] * k_ref[pl.ds(2 * u + i, 1), :])
            left = jnp.concatenate(
                [
                    jnp.concatenate([t_h, t_h], axis=1),
                    jnp.concatenate([t_l, jnp.zeros_like(t_l)], axis=1),
                ],
                axis=0,
            )
            got = dot(left, right)
            res.append(got[:32] + got[32:])
        rows = pl.ds(pl.multiple_of(u * 8, 8), 8)
        for g in range(8):
            rs[g, rows, :] = jnp.concatenate(
                [res[i][g * 4:(g + 1) * 4] for i in range(2)], axis=0
            )

    def columns(v, carry):
        grid(v, 1, 1)
        column(v, 0)
        grid(jnp.minimum(v + 1, GRID // 4 - 1), 0, 0)
        column(v, 1)
        return carry

    grid(0, 0, 0)
    lax.fori_loop(0, GRID // 4, columns, 0, unroll=8)

    def last(g, carry):
        head, tail = split(rs[g])
        res = dot(proj_ref[0], head) + (dot(proj_ref[0], tail) + dot(proj_ref[1], head))
        rows = pl.ds(pl.multiple_of(g * 128, 128), 128)
        for c in range(2):
            head, tail = split(res[:, c * 128:(c + 1) * 128])
            ks[c, rows, 0:128] = head
            ks[c, rows, 128:256] = tail
        return carry

    loads[0].wait()
    lax.fori_loop(0, 8, last, 0, unroll=4)

    def store(j):
        part = pl.ds(j * 8, 8)
        return pltpu.make_async_copy(o_ref.at[:, part], o_hbm.at[:, part], out_sems.at[j])

    def finish(j, carry):
        rows = pl.ds(pl.multiple_of(j * 256, 256), 256)
        for c in range(2):
            res = dot(back_ref[rows, :], ks[c])
            res = res[:, :128] + res[:, 128:]
            for i in range(8):
                value = res[i * 32:(i + 1) * 32] + x_ref[j * 8 + i, 2 + c]
                for g in range(8):
                    o_ref[g, j * 8 + i, c * 4:(c + 1) * 4, :] = value[g * 4:(g + 1) * 4]
        store(j).start()
        return carry

    loads[1].wait()
    lax.fori_loop(0, 4, finish, 0, unroll=2)
    for j in range(4):
        store(j).wait()


def kerr_call(received, *constants):
    vm = pl.BlockSpec(memory_space=pltpu.VMEM)
    hbm = pl.BlockSpec(memory_space=pl.ANY)
    return pl.pallas_call(
        kerr_kernel,
        name="kerr",
        out_shape=jax.ShapeDtypeStruct((ZL, 32, 8, 128), F32),
        in_specs=[vm, vm, hbm, vm, vm, hbm, vm, vm],
        out_specs=hbm,
        scratch_shapes=[
            pltpu.VMEM((4, MODES, 256), BF),
            pltpu.VMEM((4, MODES, 256), BF),
            pltpu.VMEM((4, 32, 2, 8, 8, 128), F32),
            pltpu.VMEM((8, MODES // 2, 256), F32),
            pltpu.VMEM((2, MODES, 256), BF),
            pltpu.VMEM((2, 2, 256, 256), F32),
            pltpu.VMEM((MODES, MODES), BF),
            pltpu.VMEM((MODES, MODES), BF),
            pltpu.VMEM((2, 128, MODES // 2), BF),
            pltpu.VMEM((ZL, 32, 8, 128), F32),
            pltpu.SemaphoreType.DMA((2,)),
            pltpu.SemaphoreType.DMA((4,)),
        ],
        compiler_params=pltpu.CompilerParams(vmem_limit_bytes=LIMIT),
        cost_estimate=pl.CostEstimate(flops=2 * 10**10, bytes_accessed=8 * 2**20, transcendentals=0),
    )(received, *constants)


def three(a_h, a_l, b_h, b_l):
    return dot(a_h, b_h) + (dot(a_h, b_l) + dot(a_l, b_h))


def spectral_kernel(s_ref, l_ref, ph_ref, w1_ref, w2_ref, w3_ref, w4_ref, tw_ref, o_ref, sc):
    for z in range(ZL - 1, -1, -1):
        if z == ZL - 1:
            sc[z] = s_ref[z]
        else:
            sc[z] = s_ref[z] + l_ref[z] * sc[z + 1]
    tw_r = jnp.concatenate([tw_ref[0]] * PER, axis=0)
    tw_i = jnp.concatenate([tw_ref[1]] * PER, axis=0)
    ph_r, ph_i = ph_ref[0], ph_ref[1]

    def pair(j, carry):
        z0 = 2 * j
        a = jnp.concatenate(
            [sc[z0].reshape(256, 128), sc[z0 + 1].reshape(256, 128)], axis=1
        )
        a_h, a_l = split(a)
        first = three(w1_ref[0], w1_ref[1], a_h, a_l)
        outs = []
        for i in range(2):
            re, im = first[:128, i * 128:(i + 1) * 128], first[128:, i * 128:(i + 1) * 128]
            seg = jnp.concatenate([re * tw_r - im * tw_i, re * tw_i + im * tw_r], axis=1)
            s_h, s_l = split(seg)
            spec = three(s_h, s_l, w2_ref[0], w2_ref[1])
            re, im = spec[:, :128], spec[:, 128:]
            spec = jnp.concatenate([re * ph_r - im * ph_i, re * ph_i + im * ph_r], axis=1)
            s_h, s_l = split(spec)
            seg = three(s_h, s_l, w3_ref[0], w3_ref[1])
            re, im = seg[:, :128], seg[:, 128:]
            outs.append(
                jnp.concatenate([re * tw_r + im * tw_i, im * tw_r - re * tw_i], axis=0)
            )
        b_h, b_l = split(jnp.concatenate(outs, axis=1))
        final = three(w4_ref[0], w4_ref[1], b_h, b_l)
        o_ref[z0] = final[:, :128]
        o_ref[z0 + 1] = final[:, 128:]
        return carry

    lax.fori_loop(0, ZL // 2, pair, 0, unroll=4)


def spectral_constants():
    a = np.arange(OUTER)
    ang1 = 2 * math.pi / OUTER * (np.outer(a, a) % OUTER)
    c1, s1 = np.cos(ang1), np.sin(ang1)
    eye = np.eye(PER)
    w1 = np.zeros((2, PER, OUTER, OUTER, 2, PER))
    blocks = {(0, 0): c1, (0, 1): s1, (1, 0): -s1, (1, 1): c1}
    for (co, ci), m in blocks.items():
        w1[co, :, :, :, ci, :] = np.einsum("mn,ka->mkan", eye, m)
    w1 = w1.reshape(256, 256)
    w4 = np.zeros((OUTER, 2, PER, 2, PER, OUTER))
    blocks = {(0, 0): c1, (0, 1): -s1, (1, 0): s1, (1, 1): c1}
    for (co, ci), m in blocks.items():
        w4[:, co, :, ci, :, :] = np.einsum("mn,ka->amnk", eye, m)
    w4 = w4.reshape(256, 256) / TIME
    b = np.arange(BLOCK)
    ang2 = 2 * math.pi / BLOCK * (np.outer(b, b) % BLOCK)
    c2, s2 = np.cos(ang2), np.sin(ang2)
    w2 = np.block([[c2, -s2], [s2, c2]])
    w3 = np.block([[c2, s2], [-s2, c2]])
    angt = 2 * math.pi / TIME * (np.outer(a, b) % TIME)
    tw = np.stack([np.cos(angt), -np.sin(angt)]).astype(np.float32)
    return [np.stack(halves(w)) for w in (w1, w2, w3, w4)] + [tw]


def spectral_call(source, factors, turn):
    w1, w2, w3, w4, tw = spectral_constants()
    vm = pl.BlockSpec(memory_space=pltpu.VMEM)
    return pl.pallas_call(
        spectral_kernel,
        name="spectral",
        out_shape=jax.ShapeDtypeStruct((ZL, 256, 128), F32),
        in_specs=[vm] * 8,
        out_specs=vm,
        scratch_shapes=[pltpu.VMEM((ZL, OUTER, 8, 128), F32)],
        compiler_params=pltpu.CompilerParams(vmem_limit_bytes=32 * 2**20),
        cost_estimate=pl.CostEstimate(flops=3 * 10**9, bytes_accessed=4 * 2**20, transcendentals=0),
    )(source, factors, turn, w1, w2, w3, w4, tw)


def gathered_loss(loss):
    size = lax.axis_size("gz")
    have = loss
    reach = 1
    while reach < size:
        route = [((i + reach) % size, i) for i in range(size)]
        have = jnp.concatenate([have, lax.ppermute(have, "gz", route)], axis=0)
        reach *= 2
    me = lax.axis_index("gz")
    return lax.dynamic_slice_in_dim(jnp.concatenate([have, have], axis=0), size - me, size, 0)


def kerr_tables():
    t = hermite_table()
    t_h, t_l = [part.astype(np.float64) for part in halves(t)]

    def stacked(build):
        return np.concatenate([build(t_h), build(t_h), build(t_l)], axis=1).astype(jnp.bfloat16)

    eye = np.eye(2)

    def sum_q(table):
        return np.einsum("yq,ab->yabq", table, eye).reshape(256, 64)

    def sum_p(table):
        return np.einsum("xkhp,ab->axkhbp", table.reshape(128, 8, 2, 2), eye).reshape(256, 64)

    def sum_y(table):
        return np.einsum("yq,ab->aqyb", table, np.eye(4)).reshape(128, 512)

    proj = np.stack([sum_y(t_h), sum_y(t_l)]).astype(jnp.bfloat16)
    return stacked(sum_q), stacked(sum_p), proj, np.ascontiguousarray(t.T).astype(np.float32)


def kerr_constants(mode_order, region, chi):
    f2, f3, proj, tt = kerr_tables()
    matches = (region[None, :, :] == jnp.arange(REGIONS, dtype=jnp.int32)[:, None, None]).astype(F32)
    k = 2.0 * jnp.sum(matches * chi[:, None, None], axis=0).T
    index = jnp.arange(MODES, dtype=jnp.int32)
    back = (mode_order[:, None] == index[None, :]).astype(BF)
    return mode_order[None, :], back, f2, f3, proj, tt, k


def on_device(forward, cotangent, mode_order, region, chi, phase, loss):
    me = lax.axis_index("gz")
    send = pack_call(forward, cotangent)
    received = lax.all_to_all(send, "ma", split_axis=0, concat_axis=0, tiled=True)
    constants = kerr_constants(mode_order, region, chi)
    source = kerr_call(received, *constants)
    source = source.reshape(256, 8, 128)
    gathered = lax.all_to_all(source, ("gz", "ma"), split_axis=0, concat_axis=0, tiled=True)
    factors = lax.dynamic_slice_in_dim(gathered_loss(loss), me * PER, PER, 1)
    factors = jnp.concatenate([factors, factors], axis=1)
    factors = jnp.broadcast_to(factors[:, None, :, None], (ZL, 1, 8, 128))
    angles = lax.dynamic_slice_in_dim(phase, me * PER, PER, 0)
    angles = angles.reshape(PER, BLOCK, OUTER).transpose(0, 2, 1).reshape(PER * OUTER, BLOCK)
    turn = jnp.stack([jnp.cos(angles), -jnp.sin(angles)])
    result = spectral_call(gathered.reshape(ZL, OUTER, 8, 128), factors, turn)
    result = lax.all_to_all(result, "gz", split_axis=0, concat_axis=0, tiled=True)
    result = result.reshape(8, OUTER, 2, PER, BLOCK).transpose(2, 0, 3, 1, 4)
    return result.reshape(1, 2, 32, TIME)


def solution(mesh):
    in_specs = (
        P("gz", None, "ma", None),
        P("gz", None, "ma", None),
        P(),
        P(),
        P(),
        P("ma", None),
        P("gz", "ma"),
    )
    return jax.shard_map(
        on_device, mesh=mesh, in_specs=in_specs, out_specs=P("gz", None, "ma", None), check_vma=False
    )
```

```python
import math

import jax
import jax.numpy as jnp
import numpy as np
from jax import lax
from jax.experimental import pallas as pl
from jax.experimental.pallas import tpu as pltpu
from jax.sharding import PartitionSpec as P

ORDER = 32
MODES = 1024
GRID = 128
REGIONS = 8
TIME = 4096
BLOCK = 128
OUTER = 32
ZL = 8
LIMIT = 50 * 2**20
PER = 4
BF = jnp.bfloat16
F32 = jnp.float32


def hermite_table():
    step = 20.0 / GRID
    coords = (np.arange(GRID, dtype=np.float64) - (GRID - 1) / 2.0) * step
    columns = [np.exp(-0.5 * coords * coords) * math.pi ** (-0.25)]
    columns.append(math.sqrt(2.0) * coords * columns[0])
    for n in range(2, ORDER):
        columns.append(
            math.sqrt(2.0 / n) * coords * columns[n - 1]
            - math.sqrt((n - 1.0) / n) * columns[n - 2]
        )
    return np.stack(columns, axis=1) * math.sqrt(step)


def halves(array):
    head = array.astype(jnp.bfloat16)
    tail = (array - head.astype(np.float64)).astype(jnp.bfloat16)
    return head, tail


def split(value):
    head = value.astype(BF)
    return head, (value - head.astype(F32)).astype(BF)


def dot(a, b):
    return jnp.dot(a, b, preferred_element_type=F32)


def pack_kernel(f_ref, c_ref, o_ref):
    for j in range(f_ref.shape[3] // 128):
        o_ref[j, 0:2] = f_ref[0, :, :, j * 128:(j + 1) * 128]
        o_ref[j, 2:4] = c_ref[0, :, :, j * 128:(j + 1) * 128]


def pack_call(forward, cotangent):
    steps = 2
    spec = pl.BlockSpec((1, 2, 32, TIME // steps), lambda i: (0, 0, 0, i))
    return pl.pallas_call(
        pack_kernel,
        name="pack",
        grid=(steps,),
        out_shape=jax.ShapeDtypeStruct((32, 4, 32, 128), F32),
        in_specs=[spec, spec],
        out_specs=pl.BlockSpec((32 // steps, 4, 32, 128), lambda i: (i, 0, 0, 0)),
        compiler_params=pltpu.CompilerParams(vmem_limit_bytes=60 * 2**20),
        cost_estimate=pl.CostEstimate(flops=2**20, bytes_accessed=4 * 2**20, transcendentals=0),
    )(forward, cotangent)


def kerr_kernel(x_ref, order_ref, back_hbm, f2_ref, f3_ref, proj_hbm, tt_ref, k_ref, o_hbm,
                xs, fs, gs, rs, ks, fb, place_ref, back_ref, proj_ref, o_ref, sems, out_sems):
    loads = [
        pltpu.make_async_copy(source, target, sems.at[i])
        for i, (source, target) in enumerate(
            ((proj_hbm, proj_ref), (back_hbm, back_ref))
        )
    ]
    for load in loads:
        load.start()

    def split_in(j, carry):
        rows = pl.ds(pl.multiple_of(j * 32, 32), 32)
        for f in range(4):
            head, tail = split(x_ref[j, f])
            xs[f, rows, 0:128] = head
            xs[f, rows, 128:256] = tail
        return carry

    lax.fori_loop(0, 32, split_in, 0, unroll=4)

    def place(j, carry):
        rows = pl.ds(pl.multiple_of(j * 256, 256), 256)
        index = lax.broadcasted_iota(jnp.int32, (256, MODES), 0) + j * 256
        place_ref[rows, :] = jnp.where(index == order_ref[...], 1.0, 0.0).astype(BF)
        for f in range(4):
            fs[f, rows, :] = dot(place_ref[rows, :], xs[f]).astype(BF)
        return carry

    lax.fori_loop(0, 4, place, 0, unroll=4)

    def first(k, carry):
        for pair in range(2):
            got = []
            for h in range(2):
                rows = pl.ds(pl.multiple_of(k * 128 + h * 64, 64), 64)
                a, b = fs[2 * pair, rows, :], fs[2 * pair + 1, rows, :]
                head = jnp.concatenate([a[:, :128], b[:, :128]], axis=1)
                tail = jnp.concatenate([a[:, 128:], b[:, 128:]], axis=1)
                res = dot(f2_ref[...], jnp.concatenate([head, tail, head], axis=0))
                got.append(res.reshape(32, 8, 256))
            low = jnp.concatenate([got[0][:, :4], got[1][:, :4]], axis=1)
            high = jnp.concatenate([got[0][:, 4:], got[1][:, 4:]], axis=1)
            for c in range(2):
                lanes = slice(c * 128, (c + 1) * 128)
                gs[2 * pair + c, :, 0, k] = low[:, :, lanes]
                gs[2 * pair + c, :, 1, k] = high[:, :, lanes]
        return carry

    lax.fori_loop(0, 8, first, 0, unroll=4)

    def grid(v, parity, slot):
        for pair in range(2):
            got = [split(gs[2 * pair + c, v, parity].reshape(64, 128)) for c in range(2)]
            head = jnp.concatenate([got[0][0], got[1][0]], axis=1)
            tail = jnp.concatenate([got[0][1], got[1][1]], axis=1)
            fb[slot, pair] = dot(f3_ref[...], jnp.concatenate([head, tail, head], axis=0))

    def column(v, parity):
        u = 2 * v + parity
        res = []
        for i in range(2):
            xr = slice(i * 128, (i + 1) * 128)
            er, ei = fb[parity, 0, xr, :128], fb[parity, 0, xr, 128:]
            cr, ci = fb[parity, 1, xr, :128], fb[parity, 1, xr, 128:]
            total = er * er + ei * ei
            turn = er * ci - ei * cr
            turn = turn + turn
            gr_h, gr_l = split(total * ci + turn * er)
            gi_h, gi_l = split(turn * ei - total * cr)
            right = jnp.concatenate(
                [jnp.concatenate([gr_h, gi_h], axis=1), jnp.concatenate([gr_l, gi_l], axis=1)], axis=0
            )
            t_h, t_l = split(tt_ref[...] * k_ref[pl.ds(2 * u + i, 1), :])
            left = jnp.concatenate(
                [
                    jnp.concatenate([t_h, t_h], axis=1),
                    jnp.concatenate([t_l, jnp.zeros_like(t_l)], axis=1),
                ],
                axis=0,
            )
            got = dot(left, right)
            res.append(got[:32] + got[32:])
        rows = pl.ds(pl.multiple_of(u * 8, 8), 8)
        for g in range(8):
            rs[g, rows, :] = jnp.concatenate(
                [res[i][g * 4:(g + 1) * 4] for i in range(2)], axis=0
            )

    def columns(v, carry):
        grid(v, 1, 1)
        column(v, 0)
        grid(jnp.minimum(v + 1, GRID // 4 - 1), 0, 0)
        column(v, 1)
        return carry

    grid(0, 0, 0)
    lax.fori_loop(0, GRID // 4, columns, 0, unroll=8)

    def last(g, carry):
        head, tail = split(rs[g])
        res = dot(proj_ref[0], head) + (dot(proj_ref[0], tail) + dot(proj_ref[1], head))
        rows = pl.ds(pl.multiple_of(g * 128, 128), 128)
        for c in range(2):
            head, tail = split(res[:, c * 128:(c + 1) * 128])
            ks[c, rows, 0:128] = head
            ks[c, rows, 128:256] = tail
        return carry

    loads[0].wait()
    lax.fori_loop(0, 8, last, 0, unroll=4)

    def store(j):
        part = pl.ds(j * 8, 8)
        return pltpu.make_async_copy(o_ref.at[:, part], o_hbm.at[:, part], out_sems.at[j])

    def finish(j, carry):
        rows = pl.ds(pl.multiple_of(j * 256, 256), 256)
        for c in range(2):
            res = dot(back_ref[rows, :], ks[c])
            res = res[:, :128] + res[:, 128:]
            for i in range(8):
                value = res[i * 32:(i + 1) * 32] + x_ref[j * 8 + i, 2 + c]
                for g in range(8):
                    o_ref[g, j * 8 + i, c * 4:(c + 1) * 4, :] = value[g * 4:(g + 1) * 4]
        store(j).start()
        return carry

    loads[1].wait()
    lax.fori_loop(0, 4, finish, 0, unroll=2)
    for j in range(4):
        store(j).wait()


def kerr_call(received, *constants):
    vm = pl.BlockSpec(memory_space=pltpu.VMEM)
    hbm = pl.BlockSpec(memory_space=pl.ANY)
    return pl.pallas_call(
        kerr_kernel,
        name="kerr",
        out_shape=jax.ShapeDtypeStruct((ZL, 32, 8, 128), F32),
        in_specs=[vm, vm, hbm, vm, vm, hbm, vm, vm],
        out_specs=hbm,
        scratch_shapes=[
            pltpu.VMEM((4, MODES, 256), BF),
            pltpu.VMEM((4, MODES, 256), BF),
            pltpu.VMEM((4, 32, 2, 8, 8, 128), F32),
            pltpu.VMEM((8, MODES // 2, 256), F32),
            pltpu.VMEM((2, MODES, 256), BF),
            pltpu.VMEM((2, 2, 256, 256), F32),
            pltpu.VMEM((MODES, MODES), BF),
            pltpu.VMEM((MODES, MODES), BF),
            pltpu.VMEM((2, 128, MODES // 2), BF),
            pltpu.VMEM((ZL, 32, 8, 128), F32),
            pltpu.SemaphoreType.DMA((2,)),
            pltpu.SemaphoreType.DMA((4,)),
        ],
        compiler_params=pltpu.CompilerParams(vmem_limit_bytes=LIMIT),
        cost_estimate=pl.CostEstimate(flops=2 * 10**10, bytes_accessed=8 * 2**20, transcendentals=0),
    )(received, *constants)


def three(a_h, a_l, b_h, b_l):
    return dot(a_h, b_h) + (dot(a_h, b_l) + dot(a_l, b_h))


def spectral_kernel(s_ref, l_ref, ph_ref, w1_ref, w2_ref, w3_ref, w4_ref, tw_ref, o_ref, sc):
    for z in range(ZL - 1, -1, -1):
        if z == ZL - 1:
            sc[z] = s_ref[z]
        else:
            sc[z] = s_ref[z] + l_ref[z] * sc[z + 1]
    tw_r = jnp.concatenate([tw_ref[0]] * PER, axis=0)
    tw_i = jnp.concatenate([tw_ref[1]] * PER, axis=0)
    ph_r, ph_i = ph_ref[0], ph_ref[1]

    def pair(j, carry):
        z0 = 2 * j
        a = jnp.concatenate(
            [sc[z0].reshape(256, 128), sc[z0 + 1].reshape(256, 128)], axis=1
        )
        a_h, a_l = split(a)
        first = three(w1_ref[0], w1_ref[1], a_h, a_l)
        outs = []
        for i in range(2):
            re, im = first[:128, i * 128:(i + 1) * 128], first[128:, i * 128:(i + 1) * 128]
            seg = jnp.concatenate([re * tw_r - im * tw_i, re * tw_i + im * tw_r], axis=1)
            s_h, s_l = split(seg)
            spec = three(s_h, s_l, w2_ref[0], w2_ref[1])
            re, im = spec[:, :128], spec[:, 128:]
            spec = jnp.concatenate([re * ph_r - im * ph_i, re * ph_i + im * ph_r], axis=1)
            s_h, s_l = split(spec)
            seg = three(s_h, s_l, w3_ref[0], w3_ref[1])
            re, im = seg[:, :128], seg[:, 128:]
            outs.append(
                jnp.concatenate([re * tw_r + im * tw_i, im * tw_r - re * tw_i], axis=0)
            )
        b_h, b_l = split(jnp.concatenate(outs, axis=1))
        final = three(w4_ref[0], w4_ref[1], b_h, b_l)
        o_ref[z0] = final[:, :128]
        o_ref[z0 + 1] = final[:, 128:]
        return carry

    lax.fori_loop(0, ZL // 2, pair, 0, unroll=4)


def spectral_constants():
    a = np.arange(OUTER)
    ang1 = 2 * math.pi / OUTER * (np.outer(a, a) % OUTER)
    c1, s1 = np.cos(ang1), np.sin(ang1)
    eye = np.eye(PER)
    w1 = np.zeros((2, PER, OUTER, OUTER, 2, PER))
    blocks = {(0, 0): c1, (0, 1): s1, (1, 0): -s1, (1, 1): c1}
    for (co, ci), m in blocks.items():
        w1[co, :, :, :, ci, :] = np.einsum("mn,ka->mkan", eye, m)
    w1 = w1.reshape(256, 256)
    w4 = np.zeros((OUTER, 2, PER, 2, PER, OUTER))
    blocks = {(0, 0): c1, (0, 1): -s1, (1, 0): s1, (1, 1): c1}
    for (co, ci), m in blocks.items():
        w4[:, co, :, ci, :, :] = np.einsum("mn,ka->amnk", eye, m)
    w4 = w4.reshape(256, 256) / TIME
    b = np.arange(BLOCK)
    ang2 = 2 * math.pi / BLOCK * (np.outer(b, b) % BLOCK)
    c2, s2 = np.cos(ang2), np.sin(ang2)
    w2 = np.block([[c2, -s2], [s2, c2]])
    w3 = np.block([[c2, s2], [-s2, c2]])
    angt = 2 * math.pi / TIME * (np.outer(a, b) % TIME)
    tw = np.stack([np.cos(angt), -np.sin(angt)]).astype(np.float32)
    return [np.stack(halves(w)) for w in (w1, w2, w3, w4)] + [tw]


def spectral_call(source, factors, turn):
    w1, w2, w3, w4, tw = spectral_constants()
    vm = pl.BlockSpec(memory_space=pltpu.VMEM)
    return pl.pallas_call(
        spectral_kernel,
        name="spectral",
        out_shape=jax.ShapeDtypeStruct((ZL, 256, 128), F32),
        in_specs=[vm] * 8,
        out_specs=vm,
        scratch_shapes=[pltpu.VMEM((ZL, OUTER, 8, 128), F32)],
        compiler_params=pltpu.CompilerParams(vmem_limit_bytes=32 * 2**20),
        cost_estimate=pl.CostEstimate(flops=3 * 10**9, bytes_accessed=4 * 2**20, transcendentals=0),
    )(source, factors, turn, w1, w2, w3, w4, tw)


def gathered_loss(loss):
    size = lax.axis_size("gz")
    have = loss
    reach = 1
    while reach < size:
        route = [((i + reach) % size, i) for i in range(size)]
        have = jnp.concatenate([have, lax.ppermute(have, "gz", route)], axis=0)
        reach *= 2
    me = lax.axis_index("gz")
    return lax.dynamic_slice_in_dim(jnp.concatenate([have, have], axis=0), size - me, size, 0)


def kerr_tables():
    t = hermite_table()
    t_h, t_l = [part.astype(np.float64) for part in halves(t)]

    def stacked(build):
        return np.concatenate([build(t_h), build(t_h), build(t_l)], axis=1).astype(jnp.bfloat16)

    eye = np.eye(2)

    def sum_q(table):
        return np.einsum("yq,ab->yabq", table, eye).reshape(256, 64)

    def sum_p(table):
        return np.einsum("xkhp,ab->axkhbp", table.reshape(128, 8, 2, 2), eye).reshape(256, 64)

    def sum_y(table):
        return np.einsum("yq,ab->aqyb", table, np.eye(4)).reshape(128, 512)

    proj = np.stack([sum_y(t_h), sum_y(t_l)]).astype(jnp.bfloat16)
    return stacked(sum_q), stacked(sum_p), proj, np.ascontiguousarray(t.T).astype(np.float32)


def kerr_constants(mode_order, region, chi):
    f2, f3, proj, tt = kerr_tables()
    matches = (region[None, :, :] == jnp.arange(REGIONS, dtype=jnp.int32)[:, None, None]).astype(F32)
    k = 2.0 * jnp.sum(matches * chi[:, None, None], axis=0).T
    index = jnp.arange(MODES, dtype=jnp.int32)
    back = (mode_order[:, None] == index[None, :]).astype(BF)
    return mode_order[None, :], back, f2, f3, proj, tt, k


def on_device(forward, cotangent, mode_order, region, chi, phase, loss):
    me = lax.axis_index("gz")
    send = pack_call(forward, cotangent)
    received = lax.all_to_all(send, "ma", split_axis=0, concat_axis=0, tiled=True)
    constants = kerr_constants(mode_order, region, chi)
    source = kerr_call(received, *constants)
    source = source.reshape(256, 8, 128)
    gathered = lax.all_to_all(source, ("gz", "ma"), split_axis=0, concat_axis=0, tiled=True)
    factors = lax.dynamic_slice_in_dim(gathered_loss(loss), me * PER, PER, 1)
    factors = jnp.concatenate([factors, factors], axis=1)
    factors = jnp.broadcast_to(factors[:, None, :, None], (ZL, 1, 8, 128))
    angles = lax.dynamic_slice_in_dim(phase, me * PER, PER, 0)
    angles = angles.reshape(PER, BLOCK, OUTER).transpose(0, 2, 1).reshape(PER * OUTER, BLOCK)
    turn = jnp.stack([jnp.cos(angles), -jnp.sin(angles)])
    result = spectral_call(gathered.reshape(ZL, OUTER, 8, 128), factors, turn)
    result = lax.all_to_all(result, "gz", split_axis=0, concat_axis=0, tiled=True)
    result = result.reshape(8, OUTER, 2, PER, BLOCK).transpose(2, 0, 3, 1, 4)
    return result.reshape(1, 2, 32, TIME)


def solution(mesh):
    in_specs = (
        P("gz", None, "ma", None),
        P("gz", None, "ma", None),
        P(),
        P(),
        P(),
        P("ma", None),
        P("gz", "ma"),
    )
    return jax.shard_map(
        on_device, mesh=mesh, in_specs=in_specs, out_specs=P("gz", None, "ma", None), check_vma=False
    )
```

```python
import math

import jax
import jax.numpy as jnp
import numpy as np
from jax import lax
from jax.experimental import pallas as pl
from jax.experimental.pallas import tpu as pltpu
from jax.sharding import PartitionSpec as P

ORDER = 32
MODES = 1024
GRID = 128
REGIONS = 8
TIME = 4096
BLOCK = 128
OUTER = 32
ZL = 8
LIMIT = 50 * 2**20
PER = 4
BF = jnp.bfloat16
F32 = jnp.float32


def hermite_table():
    step = 20.0 / GRID
    coords = (np.arange(GRID, dtype=np.float64) - (GRID - 1) / 2.0) * step
    columns = [np.exp(-0.5 * coords * coords) * math.pi ** (-0.25)]
    columns.append(math.sqrt(2.0) * coords * columns[0])
    for n in range(2, ORDER):
        columns.append(
            math.sqrt(2.0 / n) * coords * columns[n - 1]
            - math.sqrt((n - 1.0) / n) * columns[n - 2]
        )
    return np.stack(columns, axis=1) * math.sqrt(step)


def halves(array):
    head = array.astype(jnp.bfloat16)
    tail = (array - head.astype(np.float64)).astype(jnp.bfloat16)
    return head, tail


def split(value):
    head = value.astype(BF)
    return head, (value - head.astype(F32)).astype(BF)


def dot(a, b):
    return jnp.dot(a, b, preferred_element_type=F32)


def pack_kernel(f_ref, c_ref, o_ref):
    for j in range(f_ref.shape[3] // 128):
        o_ref[j, 0:2] = f_ref[0, :, :, j * 128:(j + 1) * 128]
        o_ref[j, 2:4] = c_ref[0, :, :, j * 128:(j + 1) * 128]


def pack_call(forward, cotangent):
    steps = 2
    spec = pl.BlockSpec((1, 2, 32, TIME // steps), lambda i: (0, 0, 0, i))
    return pl.pallas_call(
        pack_kernel,
        name="pack",
        grid=(steps,),
        out_shape=jax.ShapeDtypeStruct((32, 4, 32, 128), F32),
        in_specs=[spec, spec],
        out_specs=pl.BlockSpec((32 // steps, 4, 32, 128), lambda i: (i, 0, 0, 0)),
        compiler_params=pltpu.CompilerParams(vmem_limit_bytes=60 * 2**20),
        cost_estimate=pl.CostEstimate(flops=2**20, bytes_accessed=4 * 2**20, transcendentals=0),
    )(forward, cotangent)


def kerr_kernel(x_ref, order_ref, back_hbm, f2_ref, f3_ref, proj_hbm, tt_ref, k_ref, o_hbm,
                xs, fs, gs, rs, ks, fb, place_ref, back_ref, proj_ref, o_ref, sems, out_sems):
    loads = [
        pltpu.make_async_copy(source, target, sems.at[i])
        for i, (source, target) in enumerate(
            ((proj_hbm, proj_ref), (back_hbm, back_ref))
        )
    ]
    for load in loads:
        load.start()

    def split_in(j, carry):
        rows = pl.ds(pl.multiple_of(j * 32, 32), 32)
        for f in range(4):
            head, tail = split(x_ref[j, f])
            xs[f, rows, 0:128] = head
            xs[f, rows, 128:256] = tail
        return carry

    lax.fori_loop(0, 32, split_in, 0, unroll=4)

    def place(j, carry):
        rows = pl.ds(pl.multiple_of(j * 256, 256), 256)
        index = lax.broadcasted_iota(jnp.int32, (256, MODES), 0) + j * 256
        place_ref[rows, :] = jnp.where(index == order_ref[...], 1.0, 0.0).astype(BF)
        for f in range(4):
            fs[f, rows, :] = dot(place_ref[rows, :], xs[f]).astype(BF)
        return carry

    lax.fori_loop(0, 4, place, 0, unroll=4)

    def first(k, carry):
        for pair in range(2):
            got = []
            for h in range(2):
                rows = pl.ds(pl.multiple_of(k * 128 + h * 64, 64), 64)
                a, b = fs[2 * pair, rows, :], fs[2 * pair + 1, rows, :]
                head = jnp.concatenate([a[:, :128], b[:, :128]], axis=1)
                tail = jnp.concatenate([a[:, 128:], b[:, 128:]], axis=1)
                res = dot(f2_ref[...], jnp.concatenate([head, tail, head], axis=0))
                got.append(res.reshape(32, 8, 256))
            low = jnp.concatenate([got[0][:, :4], got[1][:, :4]], axis=1)
            high = jnp.concatenate([got[0][:, 4:], got[1][:, 4:]], axis=1)
            for c in range(2):
                lanes = slice(c * 128, (c + 1) * 128)
                gs[2 * pair + c, :, 0, k] = low[:, :, lanes]
                gs[2 * pair + c, :, 1, k] = high[:, :, lanes]
        return carry

    lax.fori_loop(0, 8, first, 0, unroll=4)

    def grid(v, parity, slot):
        for pair in range(2):
            got = [split(gs[2 * pair + c, v, parity].reshape(64, 128)) for c in range(2)]
            head = jnp.concatenate([got[0][0], got[1][0]], axis=1)
            tail = jnp.concatenate([got[0][1], got[1][1]], axis=1)
            fb[slot, pair] = dot(f3_ref[...], jnp.concatenate([head, tail, head], axis=0))

    def column(v, parity):
        u = 2 * v + parity
        res = []
        for i in range(2):
            xr = slice(i * 128, (i + 1) * 128)
            er, ei = fb[parity, 0, xr, :128], fb[parity, 0, xr, 128:]
            cr, ci = fb[parity, 1, xr, :128], fb[parity, 1, xr, 128:]
            total = er * er + ei * ei
            turn = er * ci - ei * cr
            turn = turn + turn
            gr_h, gr_l = split(total * ci + turn * er)
            gi_h, gi_l = split(turn * ei - total * cr)
            right = jnp.concatenate(
                [jnp.concatenate([gr_h, gi_h], axis=1), jnp.concatenate([gr_l, gi_l], axis=1)], axis=0
            )
            t_h, t_l = split(tt_ref[...] * k_ref[pl.ds(2 * u + i, 1), :])
            left = jnp.concatenate(
                [
                    jnp.concatenate([t_h, t_h], axis=1),
                    jnp.concatenate([t_l, jnp.zeros_like(t_l)], axis=1),
                ],
                axis=0,
            )
            got = dot(left, right)
            res.append(got[:32] + got[32:])
        rows = pl.ds(pl.multiple_of(u * 8, 8), 8)
        for g in range(8):
            rs[g, rows, :] = jnp.concatenate(
                [res[i][g * 4:(g + 1) * 4] for i in range(2)], axis=0
            )

    def columns(v, carry):
        grid(v, 1, 1)
        column(v, 0)
        grid(jnp.minimum(v + 1, GRID // 4 - 1), 0, 0)
        column(v, 1)
        return carry

    grid(0, 0, 0)
    lax.fori_loop(0, GRID // 4, columns, 0, unroll=8)

    def last(g, carry):
        head, tail = split(rs[g])
        res = dot(proj_ref[0], head) + (dot(proj_ref[0], tail) + dot(proj_ref[1], head))
        rows = pl.ds(pl.multiple_of(g * 128, 128), 128)
        for c in range(2):
            head, tail = split(res[:, c * 128:(c + 1) * 128])
            ks[c, rows, 0:128] = head
            ks[c, rows, 128:256] = tail
        return carry

    loads[0].wait()
    lax.fori_loop(0, 8, last, 0, unroll=8)

    def store(j):
        part = pl.ds(j * 8, 8)
        return pltpu.make_async_copy(o_ref.at[:, part], o_hbm.at[:, part], out_sems.at[j])

    def finish(j, carry):
        rows = pl.ds(pl.multiple_of(j * 256, 256), 256)
        for c in range(2):
            res = dot(back_ref[rows, :], ks[c])
            res = res[:, :128] + res[:, 128:]
            for i in range(8):
                value = res[i * 32:(i + 1) * 32] + x_ref[j * 8 + i, 2 + c]
                for g in range(8):
                    o_ref[g, j * 8 + i, c * 4:(c + 1) * 4, :] = value[g * 4:(g + 1) * 4]
        store(j).start()
        return carry

    loads[1].wait()
    lax.fori_loop(0, 4, finish, 0, unroll=4)
    for j in range(4):
        store(j).wait()


def kerr_call(received, *constants):
    vm = pl.BlockSpec(memory_space=pltpu.VMEM)
    hbm = pl.BlockSpec(memory_space=pl.ANY)
    return pl.pallas_call(
        kerr_kernel,
        name="kerr",
        out_shape=jax.ShapeDtypeStruct((ZL, 32, 8, 128), F32),
        in_specs=[vm, vm, hbm, vm, vm, hbm, vm, vm],
        out_specs=hbm,
        scratch_shapes=[
            pltpu.VMEM((4, MODES, 256), BF),
            pltpu.VMEM((4, MODES, 256), BF),
            pltpu.VMEM((4, 32, 2, 8, 8, 128), F32),
            pltpu.VMEM((8, MODES // 2, 256), F32),
            pltpu.VMEM((2, MODES, 256), BF),
            pltpu.VMEM((2, 2, 256, 256), F32),
            pltpu.VMEM((MODES, MODES), BF),
            pltpu.VMEM((MODES, MODES), BF),
            pltpu.VMEM((2, 128, MODES // 2), BF),
            pltpu.VMEM((ZL, 32, 8, 128), F32),
            pltpu.SemaphoreType.DMA((2,)),
            pltpu.SemaphoreType.DMA((4,)),
        ],
        compiler_params=pltpu.CompilerParams(vmem_limit_bytes=LIMIT),
        cost_estimate=pl.CostEstimate(flops=2 * 10**10, bytes_accessed=8 * 2**20, transcendentals=0),
    )(received, *constants)


def three(a_h, a_l, b_h, b_l):
    return dot(a_h, b_h) + (dot(a_h, b_l) + dot(a_l, b_h))


def spectral_kernel(s_ref, l_ref, ph_ref, w1_ref, w2_ref, w3_ref, w4_ref, tw_ref, o_ref, sc):
    for z in range(ZL - 1, -1, -1):
        if z == ZL - 1:
            sc[z] = s_ref[z]
        else:
            sc[z] = s_ref[z] + l_ref[z] * sc[z + 1]
    tw_r = jnp.concatenate([tw_ref[0]] * PER, axis=0)
    tw_i = jnp.concatenate([tw_ref[1]] * PER, axis=0)
    ph_r, ph_i = ph_ref[0], ph_ref[1]

    def pair(j, carry):
        z0 = 2 * j
        a = jnp.concatenate(
            [sc[z0].reshape(256, 128), sc[z0 + 1].reshape(256, 128)], axis=1
        )
        a_h, a_l = split(a)
        first = three(w1_ref[0], w1_ref[1], a_h, a_l)
        outs = []
        for i in range(2):
            re, im = first[:128, i * 128:(i + 1) * 128], first[128:, i * 128:(i + 1) * 128]
            seg = jnp.concatenate([re * tw_r - im * tw_i, re * tw_i + im * tw_r], axis=1)
            s_h, s_l = split(seg)
            spec = three(s_h, s_l, w2_ref[0], w2_ref[1])
            re, im = spec[:, :128], spec[:, 128:]
            spec = jnp.concatenate([re * ph_r - im * ph_i, re * ph_i + im * ph_r], axis=1)
            s_h, s_l = split(spec)
            seg = three(s_h, s_l, w3_ref[0], w3_ref[1])
            re, im = seg[:, :128], seg[:, 128:]
            outs.append(
                jnp.concatenate([re * tw_r + im * tw_i, im * tw_r - re * tw_i], axis=0)
            )
        b_h, b_l = split(jnp.concatenate(outs, axis=1))
        final = three(w4_ref[0], w4_ref[1], b_h, b_l)
        o_ref[z0] = final[:, :128]
        o_ref[z0 + 1] = final[:, 128:]
        return carry

    lax.fori_loop(0, ZL // 2, pair, 0, unroll=4)


def spectral_constants():
    a = np.arange(OUTER)
    ang1 = 2 * math.pi / OUTER * (np.outer(a, a) % OUTER)
    c1, s1 = np.cos(ang1), np.sin(ang1)
    eye = np.eye(PER)
    w1 = np.zeros((2, PER, OUTER, OUTER, 2, PER))
    blocks = {(0, 0): c1, (0, 1): s1, (1, 0): -s1, (1, 1): c1}
    for (co, ci), m in blocks.items():
        w1[co, :, :, :, ci, :] = np.einsum("mn,ka->mkan", eye, m)
    w1 = w1.reshape(256, 256)
    w4 = np.zeros((OUTER, 2, PER, 2, PER, OUTER))
    blocks = {(0, 0): c1, (0, 1): -s1, (1, 0): s1, (1, 1): c1}
    for (co, ci), m in blocks.items():
        w4[:, co, :, ci, :, :] = np.einsum("mn,ka->amnk", eye, m)
    w4 = w4.reshape(256, 256) / TIME
    b = np.arange(BLOCK)
    ang2 = 2 * math.pi / BLOCK * (np.outer(b, b) % BLOCK)
    c2, s2 = np.cos(ang2), np.sin(ang2)
    w2 = np.block([[c2, -s2], [s2, c2]])
    w3 = np.block([[c2, s2], [-s2, c2]])
    angt = 2 * math.pi / TIME * (np.outer(a, b) % TIME)
    tw = np.stack([np.cos(angt), -np.sin(angt)]).astype(np.float32)
    return [np.stack(halves(w)) for w in (w1, w2, w3, w4)] + [tw]


def spectral_call(source, factors, turn):
    w1, w2, w3, w4, tw = spectral_constants()
    vm = pl.BlockSpec(memory_space=pltpu.VMEM)
    return pl.pallas_call(
        spectral_kernel,
        name="spectral",
        out_shape=jax.ShapeDtypeStruct((ZL, 256, 128), F32),
        in_specs=[vm] * 8,
        out_specs=vm,
        scratch_shapes=[pltpu.VMEM((ZL, OUTER, 8, 128), F32)],
        compiler_params=pltpu.CompilerParams(vmem_limit_bytes=32 * 2**20),
        cost_estimate=pl.CostEstimate(flops=3 * 10**9, bytes_accessed=4 * 2**20, transcendentals=0),
    )(source, factors, turn, w1, w2, w3, w4, tw)


def gathered_loss(loss):
    size = lax.axis_size("gz")
    have = loss
    reach = 1
    while reach < size:
        route = [((i + reach) % size, i) for i in range(size)]
        have = jnp.concatenate([have, lax.ppermute(have, "gz", route)], axis=0)
        reach *= 2
    me = lax.axis_index("gz")
    return lax.dynamic_slice_in_dim(jnp.concatenate([have, have], axis=0), size - me, size, 0)


def kerr_tables():
    t = hermite_table()
    t_h, t_l = [part.astype(np.float64) for part in halves(t)]

    def stacked(build):
        return np.concatenate([build(t_h), build(t_h), build(t_l)], axis=1).astype(jnp.bfloat16)

    eye = np.eye(2)

    def sum_q(table):
        return np.einsum("yq,ab->yabq", table, eye).reshape(256, 64)

    def sum_p(table):
        return np.einsum("xkhp,ab->axkhbp", table.reshape(128, 8, 2, 2), eye).reshape(256, 64)

    def sum_y(table):
        return np.einsum("yq,ab->aqyb", table, np.eye(4)).reshape(128, 512)

    proj = np.stack([sum_y(t_h), sum_y(t_l)]).astype(jnp.bfloat16)
    return stacked(sum_q), stacked(sum_p), proj, np.ascontiguousarray(t.T).astype(np.float32)


def kerr_constants(mode_order, region, chi):
    f2, f3, proj, tt = kerr_tables()
    matches = (region[None, :, :] == jnp.arange(REGIONS, dtype=jnp.int32)[:, None, None]).astype(F32)
    k = 2.0 * jnp.sum(matches * chi[:, None, None], axis=0).T
    index = jnp.arange(MODES, dtype=jnp.int32)
    back = (mode_order[:, None] == index[None, :]).astype(BF)
    return mode_order[None, :], back, f2, f3, proj, tt, k


def on_device(forward, cotangent, mode_order, region, chi, phase, loss):
    me = lax.axis_index("gz")
    send = pack_call(forward, cotangent)
    received = lax.all_to_all(send, "ma", split_axis=0, concat_axis=0, tiled=True)
    constants = kerr_constants(mode_order, region, chi)
    source = kerr_call(received, *constants)
    source = source.reshape(256, 8, 128)
    gathered = lax.all_to_all(source, ("gz", "ma"), split_axis=0, concat_axis=0, tiled=True)
    factors = lax.dynamic_slice_in_dim(gathered_loss(loss), me * PER, PER, 1)
    factors = jnp.concatenate([factors, factors], axis=1)
    factors = jnp.broadcast_to(factors[:, None, :, None], (ZL, 1, 8, 128))
    angles = lax.dynamic_slice_in_dim(phase, me * PER, PER, 0)
    angles = angles.reshape(PER, BLOCK, OUTER).transpose(0, 2, 1).reshape(PER * OUTER, BLOCK)
    turn = jnp.stack([jnp.cos(angles), -jnp.sin(angles)])
    result = spectral_call(gathered.reshape(ZL, OUTER, 8, 128), factors, turn)
    result = lax.all_to_all(result, "gz", split_axis=0, concat_axis=0, tiled=True)
    result = result.reshape(8, OUTER, 2, PER, BLOCK).transpose(2, 0, 3, 1, 4)
    return result.reshape(1, 2, 32, TIME)


def solution(mesh):
    in_specs = (
        P("gz", None, "ma", None),
        P("gz", None, "ma", None),
        P(),
        P(),
        P(),
        P("ma", None),
        P("gz", "ma"),
    )
    return jax.shard_map(
        on_device, mesh=mesh, in_specs=in_specs, out_specs=P("gz", None, "ma", None), check_vma=False
    )
```
